512 devices in a mesh: blk: 16 (over y_lo, x), rhs: 32 (over z, y_hi, core).
Axes of the slice: x: 4, y: 8 (y_hi: 2, y_lo: 4; y = y_hi * 4 + y_lo), z: 8, core: 2. Of those that a mesh axis runs over, the one named last changes fastest.
Arguments:
- factor: bfloat16 [2, 16, 2048, 8192], P(None, 'blk', 'rhs'), as said below
- loads: float32 [2, 16, 2048, 128], P(None, 'blk', 'rhs'), may hold values from -6 to 6
Outputs:
- advanced: float32 [2, 16, 2048, 128], P(None, 'blk', 'rhs')
The draws below stay inside these ranges and needn't reach their ends.
Inputs may be any that keep to these rules, and one draw needn't show every extreme that they name: factor is block lower triangular: F_gk is zero for k > g, and each diagonal block F_kk is lower triangular with diagonal entries of 0.5 to 1.5.
All inputs are finite; a program needn't handle non-finite values.
Results may differ from the reference program's by a relative error of at most 0.002.
Values may be sent and summed in bfloat16 or wider, within the bound.
No kernel may reach another device: no remote copies, remote signals or barrier semaphores. Data moves between devices by JAX's collectives and lax.ppermute only.
A program may use at most 64 MiB of HBM per device.

```python
import jax
import jax.numpy as jnp
from jax import lax

BLOCK = 2048
STEPS = 4
ROUNDS = 2
CASES = 128
N_BLK = 16


def draw_factor(key, part):
    width = STEPS * BLOCK
    shape = (ROUNDS, N_BLK, BLOCK, width)
    key_base = jax.random.fold_in(key, 11)
    key_diag = jax.random.fold_in(key, 13)
    base = jax.random.normal(key_base, shape, jnp.float32)
    off = base * (0.7 / width ** 0.5)
    lower = base * (0.6 / BLOCK ** 0.5)
    diagv = jax.random.uniform(key_diag, shape, jnp.float32, 0.5, 1.5)
    blockrow = (jnp.arange(ROUNDS)[:, None] * N_BLK + jnp.arange(N_BLK)[None, :]).reshape(ROUNDS, N_BLK, 1, 1)
    within = jnp.arange(BLOCK).reshape(1, 1, BLOCK, 1)
    column = jnp.arange(width).reshape(1, 1, 1, width)
    colblock = column // BLOCK
    inner = column % BLOCK
    dval = jnp.where(inner == within, diagv, jnp.where(inner < within, lower, 0.0))
    values = jnp.where(colblock < blockrow, off, jnp.where(colblock == blockrow, dval, 0.0))
    return values.astype(jnp.bfloat16)


def level_of(key, dims, pieces, least, high):
    def one(dim, blocks):
        draws = jax.random.uniform(jax.random.fold_in(jax.random.fold_in(key, 6), dim), (blocks,), jnp.float32, least / len(pieces), high / len(pieces))
        return jnp.repeat(jnp.exp(draws), dims[dim] // blocks).reshape((-1,) + (1,) * (len(dims) - dim - 1))

    level = one(*pieces[0])
    for cut in pieces[1:]:
        level = level * one(*cut)
    return level


def scatter_about(key, extent, spread, reach, cuts=(), dtype=jnp.bfloat16):
    drawn = spread * jax.random.normal(key, extent, jnp.float32)
    if cuts:
        drawn = drawn * level_of(key, extent, cuts, -0.22, 0.18)
    return jnp.clip(drawn, -reach, reach).astype(dtype)


def setup_inputs(seed: int = 0) -> dict:
    key_of = jax.random.split(jax.random.key(seed), 3)
    return {
        "factor": draw_factor(jax.random.fold_in(key_of[2], 71), 0),
        "loads": scatter_about(key_of[1], (ROUNDS, N_BLK, BLOCK, CASES), 1.0, 6.0, ((1, 16), (2, 32)), jnp.float32),
    }


def reference(factor, loads):
    blocks = ROUNDS * N_BLK
    rows = factor.reshape(blocks, BLOCK, STEPS * BLOCK)
    work = loads.reshape(blocks, BLOCK, CASES)
    for step in range(STEPS):
        column = rows[:, :, step * BLOCK:(step + 1) * BLOCK]
        solution = jnp.dot(column[step].astype(jnp.float32), work[step], precision=lax.Precision.HIGHEST)
        sent = solution.astype(jnp.bfloat16)
        update = jnp.dot(column.reshape(blocks * BLOCK, BLOCK), sent, preferred_element_type=jnp.float32)
        work = work - update.reshape(blocks, BLOCK, CASES)
        work = work.at[step].set(solution)
    return work.reshape(ROUNDS, N_BLK, BLOCK, CASES)
```

```python
import jax
import jax.numpy as jnp
from jax import lax
from jax.sharding import Mesh, PartitionSpec as P

BLK = ("yl", "x")
RHS = ("z", "yh", "c")


def gather_rows(part):
    chips = lax.axis_size(("z", "yh"))
    sent = jnp.broadcast_to(part[None], (chips,) + part.shape)
    got = lax.all_to_all(sent, ("z", "yh"), 0, 0, tiled=True)
    both = lax.all_gather(got, "c", axis=1, tiled=True)
    return both.reshape(-1, part.shape[1])


def from_owner(part, owner):
    count = lax.axis_size(BLK)
    sent = jnp.broadcast_to(part[None], (count,) + part.shape)
    return lax.all_to_all(sent, BLK, 0, 0, tiled=True)[owner]


def body(factor, loads):
    position = lax.axis_index(BLK)
    stored = factor[:, 0]
    work = loads[:, 0]
    rounds, share, width = stored.shape
    block = share * lax.axis_size(RHS)
    cycle = lax.axis_size(BLK)
    for step in range(width // block):
        owner = step % cycle
        index = step // cycle
        columns = slice(step * block, (step + 1) * block)
        diagonal = stored[index, :, columns].astype(jnp.float32)
        whole_work = gather_rows(work[index])
        solution = jnp.dot(diagonal, whole_work, precision=lax.Precision.HIGHEST)
        sent = from_owner(solution.astype(jnp.bfloat16), owner)
        whole = gather_rows(sent)
        panel = stored[:, :, columns].reshape(rounds * share, block)
        update = jnp.dot(panel, whole, preferred_element_type=jnp.float32)
        lowered = work - update.reshape(work.shape)
        work = jnp.where(position == owner, lowered.at[index].set(solution), lowered)
    return work[:, None]


def solution(mesh):
    fine = Mesh(mesh.devices.reshape(4, 4, 8, 2, 2), BLK + RHS)
    spec = P(None, BLK, RHS, None)
    return jax.shard_map(
        body, mesh=fine, in_specs=(spec, spec), out_specs=spec, check_vma=False
    )
```

```python
import jax
import jax.numpy as jnp
from jax import lax
from jax.sharding import Mesh, PartitionSpec as P

BLK = ("yl", "x")
RHS = ("z", "yh", "c")
CHIPS = ("z", "yh")


def exchange(parts, axis):
    return lax.all_to_all(parts, axis, 0, 0, tiled=True)


def repeat(part, count):
    return jnp.broadcast_to(part[None], (count,) + part.shape)


def gather_chips(part):
    got = exchange(repeat(part, lax.axis_size(CHIPS)), CHIPS)
    return jnp.swapaxes(got, 0, 1).reshape(part.shape[0], -1)


def times(values, rows):
    return lax.dot_general(
        values, rows, (((1,), (1,)), ((), ())), preferred_element_type=jnp.float32
    )


def times_exact(values, rows):
    first = lax.reduce_precision(values, 8, 7)
    rest = values - first
    second = lax.reduce_precision(rest, 8, 7)
    third = rest - second
    terms = jnp.concatenate([first, second, third], 0).astype(jnp.bfloat16)
    a, b, c = jnp.split(times(terms, rows), 3, 0)
    return (c + b) + a


def body(factor, loads):
    xs, ys = lax.axis_size("x"), lax.axis_size("yl")
    cores = lax.axis_size("c")
    stored, given = factor[:, 0], loads[:, 0]
    share, width = stored.shape[1:]
    cases = given.shape[2]
    block = share * lax.axis_size(RHS)
    steps = width // block
    half = width // 2
    few = cases // (xs * cores)
    pair = cores * share

    start = lax.all_gather(stored[0, :, :block], "c", axis=0, tiled=True)
    left = lax.all_gather(stored[0, :, :half], ("x", "c"), axis=0)
    right = lax.all_gather(stored[0, :, half:], ("x", "c"), axis=0)
    below = lax.all_gather(stored[1], ("x", "c"), axis=0)
    left, right = left.reshape(xs, pair, half), right.reshape(xs, pair, half)

    def panel(row, column):
        source = left if column * block < half else right
        place = (column * block) % half
        return source[row, :, place : place + block]

    together = lax.all_gather(given[0], "c", axis=0, tiled=True).T
    mine = lax.dynamic_index_in_dim(
        together.reshape(xs, cores, few, pair), lax.axis_index("c"), 1, False
    )
    mine = mine.reshape(xs * few, pair)
    first = times_exact(gather_chips(mine), start)
    first = jnp.where(lax.axis_index("x") == 0, first, mine)
    state = list(exchange(first.reshape(xs, few, pair), "x"))

    sent = [state[0].astype(jnp.bfloat16)]
    for step in range(1, steps):
        whole = gather_chips(sent[step - 1])
        for row in range(step, steps):
            state[row] = state[row] - times(whole, panel(row, step - 1))
        state[step] = times_exact(gather_chips(state[step]), panel(step, step))
        sent.append(state[step].astype(jnp.bfloat16))

    shared = exchange(repeat(jnp.stack(sent), ys), "yl")[0]
    got = exchange(repeat(shared, lax.axis_size(CHIPS)), CHIPS)
    whole = got.transpose(2, 1, 0, 3).reshape(few, width)
    upper = times(whole[:, :half], left.reshape(xs * pair, half)) + times(
        whole[:, half:], right.reshape(xs * pair, half)
    )
    lower = times(whole, below.reshape(xs * pair, width))
    upper = jnp.swapaxes(upper.reshape(few, xs, pair), 0, 1)
    lower = jnp.swapaxes(lower.reshape(few, xs, pair), 0, 1)
    solved = lax.axis_index("yl") == 0
    upper = jnp.where(solved, jnp.stack(state), upper)
    both = jnp.stack([upper, lower], 1)[:, None]
    both = jnp.broadcast_to(both, (xs, cores) + both.shape[2:])
    both = both.reshape((xs * cores,) + both.shape[2:])
    back = exchange(both, ("x", "c"))
    back = jnp.swapaxes(back, 0, 1).reshape(2, cases, pair).transpose(0, 2, 1)
    back = lax.dynamic_slice_in_dim(back, lax.axis_index("c") * share, share, 1)
    top = jnp.where(solved, back[0], given[0] - back[0])
    return jnp.stack([top, given[1] - back[1]])[:, None]


def solution(mesh):
    fine = Mesh(mesh.devices.reshape(4, 4, 8, 2, 2), BLK + RHS)
    spec = P(None, BLK, RHS, None)
    return jax.shard_map(
        body, mesh=fine, in_specs=(spec, spec), out_specs=spec, check_vma=False
    )
```

```python
import jax
import jax.numpy as jnp
from jax import lax
from jax.sharding import Mesh, PartitionSpec as P

BLK = ("yl", "x")
RHS = ("z", "yh", "c")
CHIPS = ("z", "yh")


def exchange(parts, axis):
    return lax.all_to_all(parts, axis, 0, 0, tiled=True)


def repeat(part, count):
    return jnp.broadcast_to(part[None], (count,) + part.shape)


def gather_chips(part):
    got = exchange(repeat(part, lax.axis_size(CHIPS)), CHIPS)
    return jnp.swapaxes(got, 0, 1).reshape(part.shape[0], -1)


def times(values, rows):
    return lax.dot_general(
        values, rows, (((1,), (1,)), ((), ())), preferred_element_type=jnp.float32
    )


def times_exact(values, rows):
    first = lax.reduce_precision(values, 8, 7)
    rest = values - first
    second = lax.reduce_precision(rest, 8, 7)
    third = rest - second
    terms = jnp.concatenate([first, second, third], 0).astype(jnp.bfloat16)
    a, b, c = jnp.split(times(terms, rows), 3, 0)
    return (c + b) + a


def body(factor, loads):
    xs, ys = lax.axis_size("x"), lax.axis_size("yl")
    cores = lax.axis_size("c")
    stored, given = factor[:, 0], loads[:, 0]
    share, width = stored.shape[1:]
    cases = given.shape[2]
    block = share * lax.axis_size(RHS)
    steps = width // block
    half = width // 2
    few = cases // (xs * cores)
    pair = cores * share

    def rows_of_line(part):
        return lax.all_gather(part, ("x", "c"), axis=0).reshape(
            xs, cores * part.shape[0], part.shape[1]
        )

    def after(value, done):
        return lax.optimization_barrier((value, done))[0][:, 0]

    columns = [rows_of_line(stored[0, :, :block])]

    together = lax.all_gather(given[0], "c", axis=0, tiled=True).T
    mine = lax.dynamic_index_in_dim(
        together.reshape(xs, cores, few, pair), lax.axis_index("c"), 1, False
    )
    state = list(exchange(mine, "x"))
    columns.append(rows_of_line(after(factor, state[0])[0, :, block:half]))
    whole = gather_chips(state[0])
    last = rows_of_line(after(factor, whole)[0, :, half:])
    columns += [last[:, :, :block], last[:, :, block:]]
    sent = []
    for step in range(steps):
        state[step] = times_exact(whole, columns[step][step])
        sent.append(state[step].astype(jnp.bfloat16))
        if step + 1 == steps:
            break
        whole = gather_chips(sent[step])
        if step == 0:
            below = rows_of_line(after(factor, whole)[1])
        for row in range(step + 1, steps):
            state[row] = state[row] - times(whole, columns[step][row])
        whole = gather_chips(state[step + 1])

    shared = exchange(repeat(jnp.stack(sent), ys), "yl")[0]
    got = exchange(repeat(shared, lax.axis_size(CHIPS)), CHIPS)
    whole = got.transpose(2, 1, 0, 3).reshape(few, width)
    upper = times(whole[:, half:], last.reshape(xs * pair, half))
    for index in range(2):
        part = whole[:, index * block : (index + 1) * block]
        upper += times(part, columns[index].reshape(xs * pair, block))
    lower = times(whole, below.reshape(xs * pair, width))
    upper = jnp.swapaxes(upper.reshape(few, xs, pair), 0, 1)
    lower = jnp.swapaxes(lower.reshape(few, xs, pair), 0, 1)
    solved = lax.axis_index("yl") == 0
    upper = jnp.where(solved, jnp.stack(state), upper)
    both = jnp.stack([upper, lower], 1)[:, None]
    both = jnp.broadcast_to(both, (xs, cores) + both.shape[2:])
    both = both.reshape((xs * cores,) + both.shape[2:])
    back = exchange(both, ("x", "c"))
    back = jnp.swapaxes(back, 0, 1).reshape(2, cases, pair).transpose(0, 2, 1)
    back = lax.dynamic_slice_in_dim(back, lax.axis_index("c") * share, share, 1)
    top = jnp.where(solved, back[0], given[0] - back[0])
    return jnp.stack([top, given[1] - back[1]])[:, None]


def solution(mesh):
    fine = Mesh(mesh.devices.reshape(4, 4, 8, 2, 2), BLK + RHS)
    spec = P(None, BLK, RHS, None)
    return jax.shard_map(
        body, mesh=fine, in_specs=(spec, spec), out_specs=spec, check_vma=False
    )
```

```python
import jax
import jax.numpy as jnp
from jax import lax
from jax.sharding import Mesh, PartitionSpec as P

BLK = ("yl", "x")
RHS = ("z", "yh", "c")
CHIPS = ("z", "yh")


def exchange(parts, axis):
    return lax.all_to_all(parts, axis, 0, 0, tiled=True)


def repeat(part, count):
    return jnp.broadcast_to(part[None], (count,) + part.shape)


def gather_chips(part):
    got = exchange(repeat(part, lax.axis_size(CHIPS)), CHIPS)
    return jnp.swapaxes(got, 0, 1).reshape(part.shape[0], -1)


def times(values, rows):
    return lax.dot_general(
        values, rows, (((1,), (1,)), ((), ())), preferred_element_type=jnp.float32
    )


def times_exact(values, rows):
    first = lax.reduce_precision(values, 8, 7)
    rest = values - first
    second = lax.reduce_precision(rest, 8, 7)
    third = rest - second
    terms = jnp.concatenate([first, second, third], 0).astype(jnp.bfloat16)
    a, b, c = jnp.split(times(terms, rows), 3, 0)
    return (c + b) + a


def body(factor, loads):
    xs, cores = lax.axis_size("x"), lax.axis_size("c")
    stored, given = factor[:, 0], loads[:, 0]
    share, width = stored.shape[1:]
    cases = given.shape[2]
    block = share * lax.axis_size(RHS)
    steps = width // block
    half = width // 2
    few = cases // (xs * cores)
    pair = cores * share

    def rows_of_line(part):
        return lax.all_gather(part, ("x", "c"), axis=0).reshape(
            xs, cores * part.shape[0], part.shape[1]
        )

    left = rows_of_line(stored[0, :, :half])

    together = lax.all_gather(given[0], "c", axis=0, tiled=True).T
    mine = lax.dynamic_index_in_dim(
        together.reshape(xs, cores, few, pair), lax.axis_index("c"), 1, False
    )
    mine = mine.reshape(xs * few, pair)
    def column(step):
        source = left if step * block < half else right
        place = (step * block) % half
        return source[:, :, place : place + block]

    start = lax.all_gather(stored[0, :, :block], "c", axis=0, tiled=True)
    whole = gather_chips(mine)
    first = times_exact(whole, start)
    first = jnp.where(lax.axis_index("x") == 0, first, mine)
    state = exchange(first.reshape(xs, few, pair), "x")

    none = jnp.minimum(jnp.abs(first[0, 0]), 0.0).astype(jnp.int32)
    right = rows_of_line(lax.dynamic_slice_in_dim(stored[0], half + none, half, 1))
    below = rows_of_line(lax.dynamic_index_in_dim(stored, 1 + none, 0, False))

    solved, sent = [state[0]], [state[0].astype(jnp.bfloat16)]
    state = state[1:]
    for step in range(1, steps):
        whole = gather_chips(sent[-1])
        rows = column(step - 1)[step:].reshape(-1, block)
        update = times(whole, rows).reshape(few, steps - step, pair)
        state = state - jnp.swapaxes(update, 0, 1)
        solved.append(times_exact(gather_chips(state[0]), column(step)[step]))
        sent.append(solved[-1].astype(jnp.bfloat16))
        state = state[1:]

    height = ("yl", "yh")
    halves = lax.axis_size("yh")
    shared = jnp.concatenate(sent, 0)
    shared = exchange(repeat(shared, lax.axis_size(height)), height)[:halves]
    shared = shared.reshape(-1, pair)
    got = exchange(repeat(shared, lax.axis_size("z")), "z")
    got = got.reshape(-1, halves, steps, few, pair)
    whole = got.transpose(3, 2, 0, 1, 4).reshape(few, width)
    upper = times(whole[:, :half], left.reshape(xs * pair, half)) + times(
        whole[:, half:], right.reshape(xs * pair, half)
    )
    lower = times(whole, below.reshape(xs * pair, width))
    upper = jnp.swapaxes(upper.reshape(few, xs, pair), 0, 1)
    lower = jnp.swapaxes(lower.reshape(few, xs, pair), 0, 1)
    owner = lax.axis_index("yl") == 0
    upper = jnp.where(owner, jnp.stack(solved), upper)
    both = jnp.stack([upper, lower], 1)[:, None]
    both = jnp.broadcast_to(both, (xs, cores) + both.shape[2:])
    both = both.reshape((xs * cores,) + both.shape[2:])
    back = exchange(both, ("x", "c"))
    back = jnp.swapaxes(back, 0, 1).reshape(2, cases, pair).transpose(0, 2, 1)
    back = lax.dynamic_slice_in_dim(back, lax.axis_index("c") * share, share, 1)
    top = jnp.where(owner, back[0], given[0] - back[0])
    return jnp.stack([top, given[1] - back[1]])[:, None]


def solution(mesh):
    fine = Mesh(mesh.devices.reshape(4, 4, 8, 2, 2), BLK + RHS)
    spec = P(None, BLK, RHS, None)
    return jax.shard_map(
        body, mesh=fine, in_specs=(spec, spec), out_specs=spec, check_vma=False
    )
```

```python
import functools

import jax
import jax.numpy as jnp
from jax import lax
from jax.experimental import pallas as pl
from jax.experimental.pallas import tpu as pltpu
from jax.sharding import Mesh, PartitionSpec as P

BLK = ("yl", "x")
RHS = ("z", "yh", "c")
CHIPS = ("z", "yh")


def exchange(parts, axis):
    return lax.all_to_all(parts, axis, 0, 0, tiled=True)


def repeat(part, count):
    return jnp.broadcast_to(part[None], (count,) + part.shape)


def gather_chips(part):
    got = exchange(repeat(part, lax.axis_size(CHIPS)), CHIPS)
    return jnp.swapaxes(got, 0, 1).reshape(part.shape[0], -1)


def times(values, rows):
    return lax.dot_general(
        values, rows, (((1,), (1,)), ((), ())), preferred_element_type=jnp.float32
    )


def times_exact(values, rows):
    first = lax.reduce_precision(values, 8, 7)
    rest = values - first
    second = lax.reduce_precision(rest, 8, 7)
    third = rest - second
    terms = jnp.concatenate([first, second, third], 0).astype(jnp.bfloat16)
    a, b, c = jnp.split(times(terms, rows), 3, 0)
    return (c + b) + a


TILE, SLOTS = 1024, 6


def spread_kernel(plan, whole_ref, early_ref, all_ref, out_ref, held, sems):
    def copy(n):
        source, index, place, _ = plan[n]
        ref = (all_ref if source else early_ref).at[:, index, :, place : place + TILE]
        return pltpu.make_async_copy(ref, held.at[n % SLOTS], sems.at[n % SLOTS])

    for n in range(SLOTS):
        copy(n).start()
    total = [None, None]
    for n, (_, index, _, column) in enumerate(plan):
        copy(n).wait()
        rows = held[n % SLOTS].reshape(-1, TILE)
        part = times(whole_ref[:, column : column + TILE], rows)
        total[index] = part if total[index] is None else total[index] + part
        if n + SLOTS < len(plan):
            copy(n + SLOTS).start()
    for index in range(2):
        out_ref[index] = total[index]


def spread(whole, early, everything):
    few, width = whole.shape
    lines, _, share, wide = early.shape
    plan = [(0, 0, place, place) for place in range(0, wide, TILE)]
    plan += [(1, 0, place, place) for place in range(wide, width, TILE)]
    plan += [(1, 1, place, place) for place in range(0, width, TILE)]
    count = 2 * lines * share * width
    return pl.pallas_call(
        functools.partial(spread_kernel, plan),
        out_shape=jax.ShapeDtypeStruct((2, few, lines * share), jnp.float32),
        in_specs=[
            pl.BlockSpec(memory_space=pltpu.VMEM),
            pl.BlockSpec(memory_space=pl.ANY),
            pl.BlockSpec(memory_space=pl.ANY),
        ],
        out_specs=pl.BlockSpec(memory_space=pltpu.VMEM),
        scratch_shapes=[
            pltpu.VMEM((SLOTS, lines, share, TILE), jnp.bfloat16),
            pltpu.SemaphoreType.DMA((SLOTS,)),
        ],
        compiler_params=pltpu.CompilerParams(vmem_limit_bytes=60 * 2**20),
        cost_estimate=pl.CostEstimate(
            flops=2 * few * count, bytes_accessed=2 * count, transcendentals=0
        ),
    )(whole, early, everything)


def body(factor, loads):
    xs, cores = lax.axis_size("x"), lax.axis_size("c")
    stored, given = factor[:, 0], loads[:, 0]
    share, width = stored.shape[1:]
    cases = given.shape[2]
    block = share * lax.axis_size(RHS)
    steps = width // block
    few = cases // (xs * cores)
    pair = cores * share

    wide = 3 * block
    early = lax.all_gather(factor[:1, 0, :, :wide], ("x", "c"), axis=0)
    everything = lax.all_gather(stored, ("x", "c"), axis=0)

    def panel(row, column):
        if column * block < wide:
            source = early[:, 0, :, column * block : (column + 1) * block]
        else:
            source = everything[:, 0, :, column * block : (column + 1) * block]
        return source.reshape(xs, pair, block)[row:].reshape(-1, block)

    together = lax.all_gather(given[0], "c", axis=0, tiled=True).T
    mine = lax.dynamic_index_in_dim(
        together.reshape(xs, cores, few, pair), lax.axis_index("c"), 1, False
    )
    mine = mine.reshape(xs * few, pair)
    start = lax.all_gather(stored[0, :, :block], "c", axis=0, tiled=True)
    whole = gather_chips(mine)
    first = times_exact(whole, start)
    first = jnp.where(lax.axis_index("x") == 0, first, mine)
    state = exchange(first.reshape(xs, few, pair), "x")

    solved, sent = [state[0]], [state[0].astype(jnp.bfloat16)]
    state = state[1:]
    for step in range(1, steps):
        whole = gather_chips(sent[-1])
        update = times(whole, panel(step, step - 1))
        update = update.reshape(few, steps - step, pair)
        state = state - jnp.swapaxes(update, 0, 1)
        solved.append(times_exact(gather_chips(state[0]), panel(step, step)[:pair]))
        sent.append(solved[-1].astype(jnp.bfloat16))
        state = state[1:]

    shared = jnp.concatenate(sent, 0)
    shared = exchange(repeat(shared, lax.axis_size("yl")), "yl")[0]
    got = exchange(repeat(shared, lax.axis_size(CHIPS)), CHIPS)
    got = got.reshape(-1, steps, few, pair)
    whole = got.transpose(2, 1, 0, 3).reshape(few, width)
    update = spread(whole, early, everything)
    upper, lower = jnp.swapaxes(update.reshape(2, few, xs, pair), 1, 2)
    owner = lax.axis_index("yl") == 0
    upper = jnp.where(owner, jnp.stack(solved), upper)
    both = jnp.stack([upper, lower], 1)[:, None]
    both = jnp.broadcast_to(both, (xs, cores) + both.shape[2:])
    both = both.reshape((xs * cores,) + both.shape[2:])
    back = exchange(both, ("x", "c"))
    back = jnp.swapaxes(back, 0, 1).reshape(2, cases, pair).transpose(0, 2, 1)
    back = lax.dynamic_slice_in_dim(back, lax.axis_index("c") * share, share, 1)
    top = jnp.where(owner, back[0], given[0] - back[0])
    return jnp.stack([top, given[1] - back[1]])[:, None]


def solution(mesh):
    fine = Mesh(mesh.devices.reshape(4, 4, 8, 2, 2), BLK + RHS)
    spec = P(None, BLK, RHS, None)
    return jax.shard_map(
        body, mesh=fine, in_specs=(spec, spec), out_specs=spec, check_vma=False
    )
```

```python
import functools

import jax
import jax.numpy as jnp
from jax import lax
from jax.experimental import pallas as pl
from jax.experimental.pallas import tpu as pltpu
from jax.sharding import Mesh, PartitionSpec as P

BLK = ("yl", "x")
RHS = ("z", "yh", "c")
CHIPS = ("z", "yh")


def exchange(parts, axis):
    return lax.all_to_all(parts, axis, 0, 0, tiled=True)


def repeat(part, count):
    return jnp.broadcast_to(part[None], (count,) + part.shape)


def gather_chips(part):
    got = exchange(repeat(part, lax.axis_size(CHIPS)), CHIPS)
    return jnp.swapaxes(got, 0, 1).reshape(part.shape[0], -1)


def times(values, rows):
    return lax.dot_general(
        values, rows, (((1,), (1,)), ((), ())), preferred_element_type=jnp.float32
    )


def times_exact(values, rows):
    first = lax.reduce_precision(values, 8, 7)
    rest = values - first
    second = lax.reduce_precision(rest, 8, 7)
    third = rest - second
    terms = jnp.concatenate([first, second, third], 0).astype(jnp.bfloat16)
    a, b, c = jnp.split(times(terms, rows), 3, 0)
    return (c + b) + a


TILE, SLOTS = 1024, 6


def stream(plan, early_ref, late_ref, held, sems, cases_of):
    def copy(n):
        index, place = plan[n]
        ref = (late_ref if index else early_ref).at[:, :, place : place + TILE]
        return pltpu.make_async_copy(ref, held.at[n % SLOTS], sems.at[n % SLOTS])

    for n in range(min(SLOTS, len(plan))):
        copy(n).start()
    total = [None, None]
    for n, (index, place) in enumerate(plan):
        copy(n).wait()
        part = times(cases_of(place), held[n % SLOTS].reshape(-1, TILE))
        total[index] = part if total[index] is None else total[index] + part
        if n + SLOTS < len(plan):
            copy(n + SLOTS).start()
    return total


def first_kernel(plan, *refs):
    *whole, early_ref, late_ref, out_ref, held, sems = refs
    block = whole[0].shape[1]

    def cases_of(place):
        start = place % block
        return whole[place // block][:, start : start + TILE]

    total = stream(plan, early_ref, late_ref, held, sems, cases_of)
    for index in range(2):
        out_ref[index] = total[index]


def last_kernel(plan, owner_ref, got, sofar, solved, early_ref, late_ref, out, held, sems):
    pair = got.shape[2]
    xs = solved.shape[0]

    def cases_of(place):
        chip = (place - plan[0][1]) // pair
        return jnp.concatenate([got[chip + n] for n in range(TILE // pair)], 1)

    total = stream(plan, early_ref, late_ref, held, sems, cases_of)
    owner = owner_ref[0] == 0
    for x in range(xs):
        for index in range(2):
            span = slice(x * pair, (x + 1) * pair)
            value = sofar[index, :, span] + total[index][:, span]
            if index == 0:
                value = jnp.where(owner, solved[x], value)
            for core in range(out.shape[0] // xs):
                out[x * (out.shape[0] // xs) + core, index] = value


def streaming(kernel, plan, early, out_shape, spaces):
    lines, share, _ = early.shape
    count = len(plan) * lines * share * TILE
    few = out_shape[-2]
    return pl.pallas_call(
        functools.partial(kernel, plan),
        out_shape=jax.ShapeDtypeStruct(out_shape, jnp.float32),
        in_specs=[pl.BlockSpec(memory_space=space) for space in spaces],
        out_specs=pl.BlockSpec(memory_space=pltpu.VMEM),
        scratch_shapes=[
            pltpu.VMEM((SLOTS, lines, share, TILE), jnp.bfloat16),
            pltpu.SemaphoreType.DMA((SLOTS,)),
        ],
        compiler_params=pltpu.CompilerParams(vmem_limit_bytes=60 * 2**20),
        cost_estimate=pl.CostEstimate(
            flops=2 * few * count, bytes_accessed=2 * count, transcendentals=0
        ),
    )


def body(factor, loads):
    xs, cores = lax.axis_size("x"), lax.axis_size("c")
    stored, given = factor[:, 0], loads[:, 0]
    share, width = stored.shape[1:]
    cases = given.shape[2]
    block = share * lax.axis_size(RHS)
    steps = width // block
    few = cases // (xs * cores)
    pair = cores * share

    early = lax.all_gather(stored[0], ("x", "c"), axis=0)
    late = lax.all_gather(stored[1], ("x", "c"), axis=0)

    def panel(row, column):
        part = early[:, :, column * block : (column + 1) * block]
        return part.reshape(xs, pair, block)[row:].reshape(-1, block)

    def to_all(part):
        planes = ("yl",) + CHIPS
        got = exchange(repeat(part, lax.axis_size(planes)), planes)
        return got[: lax.axis_size(CHIPS)]

    together = lax.all_gather(given[0], "c", axis=0, tiled=True).T
    mine = lax.dynamic_index_in_dim(
        together.reshape(xs, cores, few, pair), lax.axis_index("c"), 1, False
    )
    mine = mine.reshape(xs * few, pair)
    start = lax.all_gather(stored[0, :, :block], "c", axis=0, tiled=True)
    whole = gather_chips(mine)
    first = times_exact(whole, start)
    first = jnp.where(lax.axis_index("x") == 0, first, mine)
    state = exchange(first.reshape(xs, few, pair), "x")

    solved, known = [state[0]], []
    state = state[1:]
    for step in range(1, steps):
        got = to_all(solved[-1].astype(jnp.bfloat16))
        known.append(jnp.swapaxes(got, 0, 1).reshape(few, block))
        update = times(known[-1], panel(step, step - 1))
        update = update.reshape(few, steps - step, pair)
        state = state - jnp.swapaxes(update, 0, 1)
        solved.append(times_exact(gather_chips(state[0]), panel(step, step)[:pair]))
        state = state[1:]

    got = to_all(solved[-1].astype(jnp.bfloat16))
    plan = [
        [(index, place) for place in range(*span, TILE) for index in range(2)]
        for span in ((0, width - block), (width - block, width))
    ]
    sofar = streaming(
        first_kernel,
        plan[0],
        early,
        (2, few, xs * pair),
        [pltpu.VMEM] * len(known) + [pl.ANY] * 2,
    )(*known, early, late)
    both = streaming(
        last_kernel,
        plan[1],
        early,
        (xs * cores, 2, few, pair),
        [pltpu.SMEM] + [pltpu.VMEM] * 3 + [pl.ANY] * 2,
    )(lax.axis_index("yl")[None], got, sofar, jnp.stack(solved), early, late)
    back = exchange(both, ("x", "c"))
    owner = lax.axis_index("yl") == 0
    back = jnp.swapaxes(back, 0, 1).reshape(2, cases, pair).transpose(0, 2, 1)
    back = lax.dynamic_slice_in_dim(back, lax.axis_index("c") * share, share, 1)
    top = jnp.where(owner, back[0], given[0] - back[0])
    return jnp.stack([top, given[1] - back[1]])[:, None]


def solution(mesh):
    fine = Mesh(mesh.devices.reshape(4, 4, 8, 2, 2), BLK + RHS)
    spec = P(None, BLK, RHS, None)
    return jax.shard_map(
        body, mesh=fine, in_specs=(spec, spec), out_specs=spec, check_vma=False
    )
```

```python
import functools

import jax
import jax.numpy as jnp
from jax import lax
from jax.experimental import pallas as pl
from jax.experimental.pallas import tpu as pltpu
from jax.sharding import Mesh, PartitionSpec as P

BLK = ("yl", "x")
RHS = ("z", "yh", "c")
CHIPS = ("z", "yh")


def exchange(parts, axis):
    return lax.all_to_all(parts, axis, 0, 0, tiled=True)


def repeat(part, count):
    return jnp.broadcast_to(part[None], (count,) + part.shape)


def gather_chips(part):
    got = exchange(repeat(part, lax.axis_size(CHIPS)), CHIPS)
    return jnp.swapaxes(got, 0, 1).reshape(part.shape[0], -1)


def times(values, rows):
    return lax.dot_general(
        values, rows, (((1,), (1,)), ((), ())), preferred_element_type=jnp.float32
    )


def times_exact(values, rows):
    first = lax.reduce_precision(values, 8, 7)
    rest = values - first
    second = lax.reduce_precision(rest, 8, 7)
    third = rest - second
    terms = jnp.concatenate([first, second, third], 0).astype(jnp.bfloat16)
    a, b, c = jnp.split(times(terms, rows), 3, 0)
    return (c + b) + a


TILE, SLOTS = 1024, 6


def stream(plan, sources, held, sems, cases_of):
    def copy(n):
        index, place = plan[n]
        early, late = sources
        wide = early.shape[2]
        width = (early.shape[2] + late.shape[2]) // 2
        source = late if index or place >= wide else early
        start = place if source is early else place - wide + index * width
        ref = source.at[:, :, start : start + TILE]
        return pltpu.make_async_copy(ref, held.at[n % SLOTS], sems.at[n % SLOTS])

    for n in range(min(SLOTS, len(plan))):
        copy(n).start()
    total = [None, None]
    for n, (index, place) in enumerate(plan):
        copy(n).wait()
        part = times(cases_of(place), held[n % SLOTS].reshape(-1, TILE))
        total[index] = part if total[index] is None else total[index] + part
        if n + SLOTS < len(plan):
            copy(n + SLOTS).start()
    return total


def first_kernel(plan, *refs):
    *whole, early, late, out_ref, held, sems = refs
    block = whole[0].shape[1]

    def cases_of(place):
        start = place % block
        return whole[place // block][:, start : start + TILE]

    total = stream(plan, (early, late), held, sems, cases_of)
    for index in range(2):
        out_ref[index] = total[index]


def last_kernel(plan, owner_ref, got, sofar, solved, early, late, out, *scratch):
    held, sems = scratch
    pair = got.shape[2]
    xs = solved.shape[0] + 1

    def cases_of(place):
        chip = (place - plan[0][1]) // pair
        return jnp.concatenate([got[chip + n] for n in range(TILE // pair)], 1)

    total = stream(plan, (early, late), held, sems, cases_of)
    owner = owner_ref[0] == 0
    for x in range(xs):
        for index in range(2):
            span = slice(x * pair, (x + 1) * pair)
            value = sofar[index, :, span] + total[index][:, span]
            if index == 0 and x > 0:
                value = jnp.where(owner, solved[x - 1], value)
            for core in range(out.shape[0] // xs):
                out[x * (out.shape[0] // xs) + core, index] = value


def streaming(kernel, plan, sources, out_shape, spaces):
    lines, share, _ = sources[0].shape
    count = len(plan) * lines * share * TILE
    few = out_shape[-2]
    return pl.pallas_call(
        functools.partial(kernel, plan),
        out_shape=jax.ShapeDtypeStruct(out_shape, jnp.float32),
        in_specs=[pl.BlockSpec(memory_space=space) for space in spaces],
        out_specs=pl.BlockSpec(memory_space=pltpu.VMEM),
        scratch_shapes=[
            pltpu.VMEM((SLOTS, lines, share, TILE), jnp.bfloat16),
            pltpu.SemaphoreType.DMA((SLOTS,)),
        ],
        compiler_params=pltpu.CompilerParams(vmem_limit_bytes=60 * 2**20),
        cost_estimate=pl.CostEstimate(
            flops=2 * few * count, bytes_accessed=2 * count, transcendentals=0
        ),
    )


def body(factor, loads):
    xs, cores = lax.axis_size("x"), lax.axis_size("c")
    stored, given = factor[:, 0], loads[:, 0]
    share, width = stored.shape[1:]
    cases = given.shape[2]
    block = share * lax.axis_size(RHS)
    steps = width // block
    few = cases // (xs * cores)
    pair = cores * share

    wide = width - block
    early = lax.all_gather(stored[0, :, :wide], ("x", "c"), axis=0)
    late = jnp.concatenate([stored[0, :, wide:], stored[1]], 1)
    late = lax.all_gather(late, ("x", "c"), axis=0)

    def panel(row, column):
        start = column * block
        part = late[:, :, :block] if start == wide else early[:, :, start : start + block]
        return part.reshape(xs, pair, block)[row:].reshape(-1, block)

    chips = lax.axis_size(CHIPS)

    def to_all(part):
        planes = ("yl",) + CHIPS
        got = exchange(repeat(part, lax.axis_size(planes)), planes)
        return got[:chips]

    together = lax.all_gather(given[0], "c", axis=0, tiled=True).T
    mine = lax.dynamic_index_in_dim(
        together.reshape(xs, cores, few, pair), lax.axis_index("c"), 1, False
    )
    mine = mine.reshape(xs * few, pair)
    start = lax.all_gather(stored[0, :, :block], "c", axis=0, tiled=True)
    whole = gather_chips(mine)
    state = lax.all_gather(mine, "x", axis=0).reshape(xs, xs, few, pair)[1:]
    state = lax.dynamic_index_in_dim(state, lax.axis_index("x"), 1, False)
    first = times_exact(whole, start)
    opened = lax.all_gather(first.reshape(xs, few, pair), "c", axis=1)
    opened = opened.reshape(cases, pair).T
    parts = first.astype(jnp.bfloat16).reshape(xs, 1, few, pair)
    parts = jnp.broadcast_to(parts, (xs, chips, few, pair))
    got = exchange(parts.reshape(xs * chips, few, pair), ("x",) + CHIPS)[:chips]
    whole = jnp.swapaxes(got, 0, 1).reshape(few, block)

    solved, known = [], []
    sent = [lax.dynamic_index_in_dim(got, lax.axis_index(CHIPS), 0, False)]
    for step in range(1, steps):
        update = times(whole, panel(step, step - 1))
        update = update.reshape(few, steps - step, pair)
        state = state - jnp.swapaxes(update, 0, 1)
        solved.append(times_exact(gather_chips(state[0]), panel(step, step)[:pair]))
        state = state[1:]
        sent.append(solved[-1].astype(jnp.bfloat16))
        if step == 1:
            both = to_all(jnp.concatenate(sent, 0))
            got = both[:, few:]
            known.append(jnp.swapaxes(both[:, :few], 0, 1).reshape(few, block))
        else:
            got = to_all(sent[-1])
        if step + 1 < steps:
            whole = jnp.swapaxes(got, 0, 1).reshape(few, block)
            known.append(whole)

    plan = [
        [(index, place) for place in range(*span, TILE) for index in range(2)]
        for span in ((0, width - block), (width - block, width))
    ]
    gathered = [early, late]
    sofar = streaming(
        first_kernel,
        plan[0],
        gathered,
        (2, few, xs * pair),
        [pltpu.VMEM] * len(known) + [pl.ANY] * 2,
    )(*known, *gathered)
    both = streaming(
        last_kernel,
        plan[1],
        gathered,
        (xs * cores, 2, few, pair),
        [pltpu.SMEM] + [pltpu.VMEM] * 3 + [pl.ANY] * 2,
    )(lax.axis_index("yl")[None], got, sofar, jnp.stack(solved), *gathered)
    back = exchange(both, ("x", "c"))
    owner = lax.axis_index("yl") == 0
    back = jnp.swapaxes(back, 0, 1).reshape(2, cases, pair).transpose(0, 2, 1)
    place = lax.axis_index("c") * share
    back = lax.dynamic_slice_in_dim(back, place, share, 1)
    opened = lax.dynamic_slice_in_dim(opened, place, share, 0)
    result = jnp.where(lax.axis_index("x") == 0, opened, back[0])
    top = jnp.where(owner, result, given[0] - back[0])
    return jnp.stack([top, given[1] - back[1]])[:, None]


def solution(mesh):
    fine = Mesh(mesh.devices.reshape(4, 4, 8, 2, 2), BLK + RHS)
    spec = P(None, BLK, RHS, None)
    return jax.shard_map(
        body, mesh=fine, in_specs=(spec, spec), out_specs=spec, check_vma=False
    )
```

```python
import functools

import jax
import jax.numpy as jnp
from jax import lax
from jax.experimental import pallas as pl
from jax.experimental.pallas import tpu as pltpu
from jax.sharding import Mesh, PartitionSpec as P

BLK = ("yl", "x")
RHS = ("z", "yh", "c")
CHIPS = ("z", "yh")


def exchange(parts, axis):
    return lax.all_to_all(parts, axis, 0, 0, tiled=True)


def repeat(part, count):
    return jnp.broadcast_to(part[None], (count,) + part.shape)


def times(values, rows):
    return lax.dot_general(
        values, rows, (((1,), (1,)), ((), ())), preferred_element_type=jnp.float32
    )


def times_exact(values, rows):
    first = lax.reduce_precision(values, 8, 7)
    rest = values - first
    second = lax.reduce_precision(rest, 8, 7)
    third = rest - second
    terms = jnp.concatenate([first, second, third], 0).astype(jnp.bfloat16)
    a, b, c = jnp.split(times(terms, rows), 3, 0)
    return (c + b) + a


TILE, SLOTS = 1024, 6


def stream(plan, sources, held, sems, cases_of):
    width = sum(source.shape[2] for source in sources) // 2

    def copy(n):
        index, place = plan[n]
        start = place + index * width
        for source in sources:
            if start < source.shape[2]:
                break
            start -= source.shape[2]
        ref = source.at[:, :, start : start + TILE]
        return pltpu.make_async_copy(ref, held.at[n % SLOTS], sems.at[n % SLOTS])

    for n in range(min(SLOTS, len(plan))):
        copy(n).start()
    total = [None, None]
    for n, (index, place) in enumerate(plan):
        copy(n).wait()
        part = times(cases_of(place), held[n % SLOTS].reshape(-1, TILE))
        total[index] = part if total[index] is None else total[index] + part
        if n + SLOTS < len(plan):
            copy(n + SLOTS).start()
    return total


def first_kernel(plan, *refs):
    whole, sources, (out_ref, held, sems) = refs[:3], refs[3:-3], refs[-3:]
    block = whole[0].shape[1]

    def cases_of(place):
        start = place % block
        return whole[place // block][:, start : start + TILE]

    total = stream(plan, sources, held, sems, cases_of)
    for index in range(2):
        out_ref[index] = total[index]


def last_kernel(plan, owner_ref, got, sofar, solved, *refs):
    sources, (out, held, sems) = refs[:-3], refs[-3:]
    pair = got.shape[2]
    xs = solved.shape[0]

    def cases_of(place):
        chip = (place - plan[0][1]) // pair
        return jnp.concatenate([got[chip + n] for n in range(TILE // pair)], 1)

    total = stream(plan, sources, held, sems, cases_of)
    owner = owner_ref[0] == 0
    for x in range(xs):
        for index in range(2):
            span = slice(x * pair, (x + 1) * pair)
            value = sofar[index, :, span] + total[index][:, span]
            if index == 0:
                value = jnp.where(owner, solved[x], value)
            for core in range(out.shape[0] // xs):
                out[x * (out.shape[0] // xs) + core, index] = value


def streaming(kernel, plan, sources, out_shape, spaces):
    lines, share, _ = sources[0].shape
    count = len(plan) * lines * share * TILE
    few = out_shape[-2]
    return pl.pallas_call(
        functools.partial(kernel, plan),
        out_shape=jax.ShapeDtypeStruct(out_shape, jnp.float32),
        in_specs=[pl.BlockSpec(memory_space=space) for space in spaces],
        out_specs=pl.BlockSpec(memory_space=pltpu.VMEM),
        scratch_shapes=[
            pltpu.VMEM((SLOTS, lines, share, TILE), jnp.bfloat16),
            pltpu.SemaphoreType.DMA((SLOTS,)),
        ],
        compiler_params=pltpu.CompilerParams(vmem_limit_bytes=60 * 2**20),
        cost_estimate=pl.CostEstimate(
            flops=2 * few * count, bytes_accessed=2 * count, transcendentals=0
        ),
    )


def body(factor, loads):
    xs, cores = lax.axis_size("x"), lax.axis_size("c")
    stored, given = factor[:, 0], loads[:, 0]
    share, width = stored.shape[1:]
    cases = given.shape[2]
    block = share * lax.axis_size(RHS)
    steps = width // block
    few = cases // (xs * cores)
    pair = cores * share

    def rows_of_line(part):
        return lax.all_gather(part, ("x", "c"), axis=0)

    last = width - block
    gathered = [
        rows_of_line(stored[0, :, :block]),
        rows_of_line(stored[0, :, block:last]),
        rows_of_line(jnp.concatenate([stored[0, :, last:], stored[1]], 1)),
    ]

    def panel(row, column):
        source = gathered[0 if column == 0 else 1 if column < steps - 1 else 2]
        start = (column - 1) * block if 0 < column < steps - 1 else 0
        part = source[:, :, start : start + block]
        return part.reshape(xs, pair, block)[row:].reshape(-1, block)

    chips = lax.axis_size(CHIPS)

    def to_all(part):
        planes = ("yl",) + CHIPS
        got = exchange(repeat(part, lax.axis_size(planes)), planes)
        return got[:chips]

    together = lax.all_gather(given[0], "c", axis=0, tiled=True).T
    mine = lax.dynamic_index_in_dim(
        together.reshape(xs, cores, few, pair), lax.axis_index("c"), 1, False
    )
    parts = jnp.broadcast_to(mine[:, None], (xs, chips, few, pair))
    got = exchange(parts.reshape(xs * chips, few, pair), ("x",) + CHIPS)[:chips]
    state = lax.all_gather(mine, "x", axis=0)[1:]
    state = lax.dynamic_index_in_dim(state, lax.axis_index("x"), 1, False)

    solved, known = [], []
    for step in range(steps):
        whole = jnp.swapaxes(got, 0, 1).reshape(few, block)
        solved.append(times_exact(whole, panel(step, step)[:pair]))
        got = to_all(solved[-1].astype(jnp.bfloat16))
        if step + 1 == steps:
            break
        known.append(jnp.swapaxes(got, 0, 1).reshape(few, block))
        update = times(known[-1], panel(step + 1, step))
        update = update.reshape(few, steps - step - 1, pair)
        state = state - jnp.swapaxes(update, 0, 1)
        got = exchange(repeat(state[0], chips), CHIPS)
        state = state[1:]

    plan = [
        [(index, place) for place in range(*span, TILE) for index in range(2)]
        for span in ((0, width - block), (width - block, width))
    ]
    sofar = streaming(
        first_kernel,
        plan[0],
        gathered,
        (2, few, xs * pair),
        [pltpu.VMEM] * len(known) + [pl.ANY] * len(gathered),
    )(*known, *gathered)
    both = streaming(
        last_kernel,
        plan[1],
        gathered,
        (xs * cores, 2, few, pair),
        [pltpu.SMEM] + [pltpu.VMEM] * 3 + [pl.ANY] * len(gathered),
    )(lax.axis_index("yl")[None], got, sofar, jnp.stack(solved), *gathered)
    back = exchange(both, ("x", "c"))
    owner = lax.axis_index("yl") == 0
    back = jnp.swapaxes(back, 0, 1).reshape(2, cases, pair).transpose(0, 2, 1)
    place = lax.axis_index("c") * share
    back = lax.dynamic_slice_in_dim(back, place, share, 1)
    top = jnp.where(owner, back[0], given[0] - back[0])
    return jnp.stack([top, given[1] - back[1]])[:, None]


def solution(mesh):
    fine = Mesh(mesh.devices.reshape(4, 4, 8, 2, 2), BLK + RHS)
    spec = P(None, BLK, RHS, None)
    return jax.shard_map(
        body, mesh=fine, in_specs=(spec, spec), out_specs=spec, check_vma=False
    )
```

```python
import functools

import jax
import jax.numpy as jnp
from jax import lax
from jax.experimental import pallas as pl
from jax.experimental.pallas import tpu as pltpu
from jax.sharding import Mesh, PartitionSpec as P

BLK = ("yl", "x")
RHS = ("z", "yh", "c")
CHIPS = ("z", "yh")


def exchange(parts, axis):
    return lax.all_to_all(parts, axis, 0, 0, tiled=True)


def repeat(part, count):
    return jnp.broadcast_to(part[None], (count,) + part.shape)


def gather_chips(part):
    got = exchange(repeat(part, lax.axis_size(CHIPS)), CHIPS)
    return jnp.swapaxes(got, 0, 1).reshape(part.shape[0], -1)


def times(values, rows):
    return lax.dot_general(
        values, rows, (((1,), (1,)), ((), ())), preferred_element_type=jnp.float32
    )


def times_exact(values, rows):
    first = lax.reduce_precision(values, 8, 7)
    rest = values - first
    second = lax.reduce_precision(rest, 8, 7)
    third = rest - second
    terms = jnp.concatenate([first, second, third], 0).astype(jnp.bfloat16)
    a, b, c = jnp.split(times(terms, rows), 3, 0)
    return (c + b) + a


TILES = ((1024, 6), (512, 8))


def stream(plan, early_ref, late_ref, held, sems, cases_of):
    slots, tile = held.shape[0], held.shape[3]

    def copy(n):
        index, place = plan[n]
        ref = (late_ref if index else early_ref).at[:, :, place : place + tile]
        return pltpu.make_async_copy(ref, held.at[n % slots], sems.at[n % slots])

    for n in range(min(slots, len(plan))):
        copy(n).start()
    total = [None, None]
    for n, (index, place) in enumerate(plan):
        copy(n).wait()
        part = times(cases_of(place), held[n % slots].reshape(-1, tile))
        total[index] = part if total[index] is None else total[index] + part
        if n + slots < len(plan):
            copy(n + slots).start()
    return total


def first_kernel(plan, *refs):
    *whole, early_ref, late_ref, out_ref, held, sems = refs
    block = whole[0].shape[1]

    def cases_of(place):
        start = place % block
        return whole[place // block][:, start : start + held.shape[3]]

    total = stream(plan, early_ref, late_ref, held, sems, cases_of)
    for index in range(2):
        out_ref[index] = total[index]


def last_kernel(plan, owner_ref, got, sofar, solved, early_ref, late_ref, out, held, sems):
    pair = got.shape[2]
    xs = solved.shape[0]

    def cases_of(place):
        chip = (place - plan[0][1]) // pair
        return jnp.concatenate([got[chip + n] for n in range(held.shape[3] // pair)], 1)

    total = stream(plan, early_ref, late_ref, held, sems, cases_of)
    owner = owner_ref[0] == 0
    for x in range(xs):
        for index in range(2):
            span = slice(x * pair, (x + 1) * pair)
            value = sofar[index, :, span] + total[index][:, span]
            if index == 0:
                value = jnp.where(owner, solved[x], value)
            for core in range(out.shape[0] // xs):
                out[x * (out.shape[0] // xs) + core, index] = value


def streaming(kernel, span, tiles, early, out_shape, spaces):
    lines, share, _ = early.shape
    tile, slots = tiles
    plan = [(index, place) for place in range(*span, tile) for index in range(2)]
    count = len(plan) * lines * share * tile
    few = out_shape[-2]
    return pl.pallas_call(
        functools.partial(kernel, plan),
        out_shape=jax.ShapeDtypeStruct(out_shape, jnp.float32),
        in_specs=[pl.BlockSpec(memory_space=space) for space in spaces],
        out_specs=pl.BlockSpec(memory_space=pltpu.VMEM),
        scratch_shapes=[
            pltpu.VMEM((slots, lines, share, tile), jnp.bfloat16),
            pltpu.SemaphoreType.DMA((slots,)),
        ],
        compiler_params=pltpu.CompilerParams(vmem_limit_bytes=52 * 2**20),
        cost_estimate=pl.CostEstimate(
            flops=2 * few * count, bytes_accessed=2 * count, transcendentals=0
        ),
    )


def body(factor, loads):
    xs, cores = lax.axis_size("x"), lax.axis_size("c")
    stored, given = factor[:, 0], loads[:, 0]
    share, width = stored.shape[1:]
    cases = given.shape[2]
    block = share * lax.axis_size(RHS)
    steps = width // block
    few = cases // (xs * cores)
    pair = cores * share

    early = lax.all_gather(stored[0], ("x", "c"), axis=0)
    late = lax.all_gather(stored[1], ("x", "c"), axis=0)

    def panel(row, column):
        part = early[:, :, column * block : (column + 1) * block]
        return part.reshape(xs, pair, block)[row:].reshape(-1, block)

    def to_all(part, own_plane=True):
        planes = ("yl",) + CHIPS
        got = exchange(repeat(part, lax.axis_size(planes)), planes)
        return got[: lax.axis_size(CHIPS)] if own_plane else got

    together = lax.all_gather(given[0], "c", axis=0, tiled=True).T
    mine = lax.dynamic_index_in_dim(
        together.reshape(xs, cores, few, pair), lax.axis_index("c"), 1, False
    )
    mine = mine.reshape(xs * few, pair)
    start = lax.all_gather(stored[0, :, :block], "c", axis=0, tiled=True)
    whole = gather_chips(mine)
    first = times_exact(whole, start)
    first = jnp.where(lax.axis_index("x") == 0, first, mine)
    state = exchange(first.reshape(xs, few, pair), "x")

    solved, known = [state[0]], []
    state = state[1:]
    for step in range(1, steps):
        got = to_all(solved[-1].astype(jnp.bfloat16))
        known.append(jnp.swapaxes(got, 0, 1).reshape(few, block))
        update = times(known[-1], panel(step, step - 1))
        update = update.reshape(few, steps - step, pair)
        state = state - jnp.swapaxes(update, 0, 1)
        solved.append(times_exact(gather_chips(state[0]), panel(step, step)[:pair]))
        state = state[1:]

    got = to_all(solved[-1].astype(jnp.bfloat16), False)
    last = width - block
    sofar = streaming(
        first_kernel,
        (0, last),
        TILES[0],
        early,
        (2, few, xs * pair),
        [pltpu.VMEM] * len(known) + [pl.ANY] * 2,
    )(*known, early, late)
    both = streaming(
        last_kernel,
        (last, width),
        TILES[1],
        early,
        (xs * cores, 2, few, pair),
        [pltpu.SMEM] + [pltpu.VMEM] * 3 + [pl.ANY] * 2,
    )(lax.axis_index("yl")[None], got, sofar, jnp.stack(solved), early, late)
    back = exchange(both, ("x", "c"))
    owner = lax.axis_index("yl") == 0
    back = jnp.swapaxes(back, 0, 1).reshape(2, cases, pair).transpose(0, 2, 1)
    back = lax.dynamic_slice_in_dim(back, lax.axis_index("c") * share, share, 1)
    top = jnp.where(owner, back[0], given[0] - back[0])
    return jnp.stack([top, given[1] - back[1]])[:, None]


def solution(mesh):
    fine = Mesh(mesh.devices.reshape(4, 4, 8, 2, 2), BLK + RHS)
    spec = P(None, BLK, RHS, None)
    return jax.shard_map(
        body, mesh=fine, in_specs=(spec, spec), out_specs=spec, check_vma=False
    )
```

```python
import functools

import jax
import jax.numpy as jnp
from jax import lax
from jax.experimental import pallas as pl
from jax.experimental.pallas import tpu as pltpu
from jax.sharding import Mesh, PartitionSpec as P

BLK = ("yl", "x")
RHS = ("z", "yh", "c")
CHIPS = ("z", "yh")


def exchange(parts, axis):
    return lax.all_to_all(parts, axis, 0, 0, tiled=True)


def repeat(part, count):
    return jnp.broadcast_to(part[None], (count,) + part.shape)


def gather_chips(part):
    got = exchange(repeat(part, lax.axis_size(CHIPS)), CHIPS)
    return jnp.swapaxes(got, 0, 1).reshape(part.shape[0], -1)


def times(values, rows):
    return lax.dot_general(
        values, rows, (((1,), (1,)), ((), ())), preferred_element_type=jnp.float32
    )


def times_exact(values, rows):
    first = lax.reduce_precision(values, 8, 7)
    rest = values - first
    second = lax.reduce_precision(rest, 8, 7)
    third = rest - second
    terms = jnp.concatenate([first, second, third], 0).astype(jnp.bfloat16)
    a, b, c = jnp.split(times(terms, rows), 3, 0)
    return (c + b) + a


TILES = ((1024, 6), (512, 8))


def stream(plan, early_ref, all_ref, held, sems, cases_of):
    slots, tile = held.shape[0], held.shape[3]

    def copy(n):
        index, place = plan[n]
        early = index == 0 and place < early_ref.shape[2]
        ref = early_ref if early else all_ref.at[:, index]
        ref = ref.at[:, :, place : place + tile]
        return pltpu.make_async_copy(ref, held.at[n % slots], sems.at[n % slots])

    for n in range(min(slots, len(plan))):
        copy(n).start()
    total = [None, None]
    for n, (index, place) in enumerate(plan):
        copy(n).wait()
        part = times(cases_of(place), held[n % slots].reshape(-1, tile))
        total[index] = part if total[index] is None else total[index] + part
        if n + slots < len(plan):
            copy(n + slots).start()
    return total


def first_kernel(plan, *refs):
    *got, early_ref, all_ref, out_ref, held, sems = refs

    def cases_of(place):
        chips, _, pair = got[0].shape
        part, chip = got[place // (chips * pair)], place // pair % chips
        return jnp.concatenate([part[chip + n] for n in range(held.shape[3] // pair)], 1)

    total = stream(plan, early_ref, all_ref, held, sems, cases_of)
    for index in range(2):
        out_ref[index] = total[index]


def last_kernel(plan, owner_ref, got, sofar, solved, early_ref, all_ref, out, held, sems):
    pair = got.shape[2]
    xs = solved.shape[0]

    def cases_of(place):
        chip = (place - plan[0][1]) // pair
        return jnp.concatenate([got[chip + n] for n in range(held.shape[3] // pair)], 1)

    total = stream(plan, early_ref, all_ref, held, sems, cases_of)
    owner = owner_ref[0] == 0
    for x in range(xs):
        for index in range(2):
            span = slice(x * pair, (x + 1) * pair)
            value = sofar[index, :, span] + total[index][:, span]
            if index == 0:
                value = jnp.where(owner, solved[x], value)
            for core in range(out.shape[0] // xs):
                out[x * (out.shape[0] // xs) + core, index] = value


def streaming(kernel, span, tiles, early, out_shape, spaces):
    lines, share, _ = early.shape
    tile, slots = tiles
    plan = [(index, place) for place in range(*span, tile) for index in range(2)]
    count = len(plan) * lines * share * tile
    few = out_shape[-2]
    return pl.pallas_call(
        functools.partial(kernel, plan),
        out_shape=jax.ShapeDtypeStruct(out_shape, jnp.float32),
        in_specs=[pl.BlockSpec(memory_space=space) for space in spaces],
        out_specs=pl.BlockSpec(memory_space=pltpu.VMEM),
        scratch_shapes=[
            pltpu.VMEM((slots, lines, share, tile), jnp.bfloat16),
            pltpu.SemaphoreType.DMA((slots,)),
        ],
        compiler_params=pltpu.CompilerParams(vmem_limit_bytes=52 * 2**20),
        cost_estimate=pl.CostEstimate(
            flops=2 * few * count, bytes_accessed=2 * count, transcendentals=0
        ),
    )


def body(factor, loads):
    xs, cores = lax.axis_size("x"), lax.axis_size("c")
    stored, given = factor[:, 0], loads[:, 0]
    share, width = stored.shape[1:]
    cases = given.shape[2]
    block = share * lax.axis_size(RHS)
    steps = width // block
    few = cases // (xs * cores)
    pair = cores * share

    last = width - block
    early = lax.all_gather(stored[0, :, :last], ("x", "c"), axis=0)
    everything = lax.all_gather(stored, ("x", "c"), axis=0)

    def panel(row, column):
        span = slice(column * block, (column + 1) * block)
        part = early[:, :, span] if span.start < last else everything[:, 0, :, span]
        return part.reshape(xs, pair, block)[row:].reshape(-1, block)

    def to_all(part, own_plane=True):
        planes = ("yl",) + CHIPS
        got = exchange(repeat(part, lax.axis_size(planes)), planes)
        return got[: lax.axis_size(CHIPS)] if own_plane else got

    together = lax.all_gather(given[0], "c", axis=0, tiled=True).T
    mine = lax.dynamic_index_in_dim(
        together.reshape(xs, cores, few, pair), lax.axis_index("c"), 1, False
    )
    mine = mine.reshape(xs * few, pair)
    start = lax.all_gather(stored[0, :, :block], "c", axis=0, tiled=True)
    whole = gather_chips(mine)
    first = times_exact(whole, start)
    first = jnp.where(lax.axis_index("x") == 0, first, mine)
    state = exchange(first.reshape(xs, few, pair), "x")

    solved, known = [state[0]], []
    state = state[1:]
    for step in range(1, steps):
        got = to_all(solved[-1].astype(jnp.bfloat16))
        known.append(got)
        whole = jnp.swapaxes(got, 0, 1).reshape(few, block)
        update = times(whole, panel(step, step - 1))
        update = update.reshape(few, steps - step, pair)
        state = state - jnp.swapaxes(update, 0, 1)
        solved.append(times_exact(gather_chips(state[0]), panel(step, step)[:pair]))
        state = state[1:]

    got = to_all(solved[-1].astype(jnp.bfloat16), False)
    sofar = streaming(
        first_kernel,
        (0, last),
        TILES[0],
        early,
        (2, few, xs * pair),
        [pltpu.VMEM] * len(known) + [pl.ANY] * 2,
    )(*known, early, everything)
    both = streaming(
        last_kernel,
        (last, width),
        TILES[1],
        early,
        (xs * cores, 2, few, pair),
        [pltpu.SMEM] + [pltpu.VMEM] * 3 + [pl.ANY] * 2,
    )(lax.axis_index("yl")[None], got, sofar, jnp.stack(solved), early, everything)
    back = exchange(both, ("x", "c"))
    owner = lax.axis_index("yl") == 0
    back = jnp.swapaxes(back, 0, 1).reshape(2, cases, pair).transpose(0, 2, 1)
    back = lax.dynamic_slice_in_dim(back, lax.axis_index("c") * share, share, 1)
    top = jnp.where(owner, back[0], given[0] - back[0])
    return jnp.stack([top, given[1] - back[1]])[:, None]


def solution(mesh):
    fine = Mesh(mesh.devices.reshape(4, 4, 8, 2, 2), BLK + RHS)
    spec = P(None, BLK, RHS, None)
    return jax.shard_map(
        body, mesh=fine, in_specs=(spec, spec), out_specs=spec, check_vma=False
    )
```

```python
import functools

import jax
import jax.numpy as jnp
from jax import lax
from jax.experimental import pallas as pl
from jax.experimental.pallas import tpu as pltpu
from jax.sharding import Mesh, PartitionSpec as P

BLK = ("yl", "x")
RHS = ("z", "yh", "c")
CHIPS = ("z", "yh")


def exchange(parts, axis):
    return lax.all_to_all(parts, axis, 0, 0, tiled=True)


def repeat(part, count):
    return jnp.broadcast_to(part[None], (count,) + part.shape)


def gather_chips(part):
    got = exchange(repeat(part, lax.axis_size(CHIPS)), CHIPS)
    return jnp.swapaxes(got, 0, 1).reshape(part.shape[0], -1)


def times(values, rows):
    return lax.dot_general(
        values, rows, (((1,), (1,)), ((), ())), preferred_element_type=jnp.float32
    )


def times_exact(values, rows):
    first = lax.reduce_precision(values, 8, 7)
    rest = values - first
    second = lax.reduce_precision(rest, 8, 7)
    third = rest - second
    terms = jnp.concatenate([first, second, third], 0).astype(jnp.bfloat16)
    a, b, c = jnp.split(times(terms, rows), 3, 0)
    return (c + b) + a


TILES = ((1024, 6), (512, 8))


def stream(plan, early_ref, late_ref, held, sems, cases_of):
    slots, tile = held.shape[0], held.shape[3]

    def copy(n):
        index, place = plan[n]
        ref = (late_ref if index else early_ref).at[:, :, place : place + tile]
        return pltpu.make_async_copy(ref, held.at[n % slots], sems.at[n % slots])

    for n in range(min(slots, len(plan))):
        copy(n).start()
    total = [None, None]
    for n, (index, place) in enumerate(plan):
        copy(n).wait()
        part = times(cases_of(place), held[n % slots].reshape(-1, tile))
        total[index] = part if total[index] is None else total[index] + part
        if n + slots < len(plan):
            copy(n + slots).start()
    return total


def first_kernel(plan, *refs):
    got, early_ref, late_ref, out_ref, held, sems = refs

    def cases_of(place):
        _, chips, _, pair = got.shape
        part, chip = got.at[place // (chips * pair)], place // pair % chips
        return jnp.concatenate([part[chip + n] for n in range(held.shape[3] // pair)], 1)

    total = stream(plan, early_ref, late_ref, held, sems, cases_of)
    for index in range(2):
        out_ref[index] = total[index]


def last_kernel(plan, owner_ref, got, sofar, solved, early_ref, late_ref, out, held, sems):
    pair = got.shape[2]
    xs = solved.shape[0]

    def cases_of(place):
        chip = (place - plan[0][1]) // pair
        return jnp.concatenate([got[chip + n] for n in range(held.shape[3] // pair)], 1)

    total = stream(plan, early_ref, late_ref, held, sems, cases_of)
    owner = owner_ref[0] == 0
    for x in range(xs):
        for index in range(2):
            span = slice(x * pair, (x + 1) * pair)
            value = sofar[index, :, span] + total[index][:, span]
            if index == 0:
                value = jnp.where(owner, solved[x], value)
            for core in range(out.shape[0] // xs):
                out[x * (out.shape[0] // xs) + core, index] = value


def streaming(kernel, span, tiles, early, out_shape, spaces):
    lines, share, _ = early.shape
    tile, slots = tiles
    plan = [(index, place) for place in range(*span, tile) for index in range(2)]
    count = len(plan) * lines * share * tile
    few = out_shape[-2]
    return pl.pallas_call(
        functools.partial(kernel, plan),
        out_shape=jax.ShapeDtypeStruct(out_shape, jnp.float32),
        in_specs=[pl.BlockSpec(memory_space=space) for space in spaces],
        out_specs=pl.BlockSpec(memory_space=pltpu.VMEM),
        scratch_shapes=[
            pltpu.VMEM((slots, lines, share, tile), jnp.bfloat16),
            pltpu.SemaphoreType.DMA((slots,)),
        ],
        compiler_params=pltpu.CompilerParams(vmem_limit_bytes=52 * 2**20),
        cost_estimate=pl.CostEstimate(
            flops=2 * few * count, bytes_accessed=2 * count, transcendentals=0
        ),
    )


def body(factor, loads):
    xs, cores = lax.axis_size("x"), lax.axis_size("c")
    stored, given = factor[:, 0], loads[:, 0]
    share, width = stored.shape[1:]
    cases = given.shape[2]
    block = share * lax.axis_size(RHS)
    steps = width // block
    few = cases // (xs * cores)
    pair = cores * share

    last = width - block
    early = lax.all_gather(stored[0], ("x", "c"), axis=0)
    late = lax.all_gather(stored[1], ("x", "c"), axis=0)

    def panel(row, column):
        part = early[:, :, column * block : (column + 1) * block]
        return part.reshape(xs, pair, block)[row:].reshape(-1, block)

    chips = lax.axis_size(CHIPS)

    together = lax.all_gather(given[0], "c", axis=0, tiled=True).T
    mine = lax.dynamic_index_in_dim(
        together.reshape(xs, cores, few, pair), lax.axis_index("c"), 1, False
    )
    mine = mine.reshape(xs * few, pair)
    start = lax.all_gather(stored[0, :, :block], "c", axis=0, tiled=True)
    whole = gather_chips(mine)
    first = times_exact(whole, start)
    first = jnp.where(lax.axis_index("x") == 0, first, mine)
    state = exchange(first.reshape(xs, few, pair), "x")

    solved, known = [state[0]], []
    state = state[1:]
    for step in range(1, steps):
        got = exchange(repeat(solved[-1].astype(jnp.bfloat16), chips), CHIPS)
        known.append(got)
        whole = jnp.swapaxes(got, 0, 1).reshape(few, block)
        update = times(whole, panel(step, step - 1))
        update = update.reshape(few, steps - step, pair)
        state = state - jnp.swapaxes(update, 0, 1)
        solved.append(times_exact(gather_chips(state[0]), panel(step, step)[:pair]))
        state = state[1:]

    known = lax.all_gather(jnp.stack(known), "yl", axis=0)[0]
    none = jnp.minimum(jnp.abs(known[0, 0, :1].astype(jnp.float32)), 0.0)
    planes = ("yl",) + CHIPS
    got = (solved[-1] + none).astype(jnp.bfloat16)
    got = exchange(repeat(got, lax.axis_size(planes)), planes)
    sofar = streaming(
        first_kernel,
        (0, last),
        TILES[0],
        early,
        (2, few, xs * pair),
        [pltpu.VMEM] + [pl.ANY] * 2,
    )(known, early, late)
    both = streaming(
        last_kernel,
        (last, width),
        TILES[1],
        early,
        (xs * cores, 2, few, pair),
        [pltpu.SMEM] + [pltpu.VMEM] * 3 + [pl.ANY] * 2,
    )(lax.axis_index("yl")[None], got, sofar, jnp.stack(solved), early, late)
    back = exchange(both, ("x", "c"))
    owner = lax.axis_index("yl") == 0
    back = jnp.swapaxes(back, 0, 1).reshape(2, cases, pair).transpose(0, 2, 1)
    back = lax.dynamic_slice_in_dim(back, lax.axis_index("c") * share, share, 1)
    top = jnp.where(owner, back[0], given[0] - back[0])
    return jnp.stack([top, given[1] - back[1]])[:, None]


def solution(mesh):
    fine = Mesh(mesh.devices.reshape(4, 4, 8, 2, 2), BLK + RHS)
    spec = P(None, BLK, RHS, None)
    return jax.shard_map(
        body, mesh=fine, in_specs=(spec, spec), out_specs=spec, check_vma=False
    )
```

```python
import functools

import jax
import jax.numpy as jnp
from jax import lax
from jax.experimental import pallas as pl
from jax.experimental.pallas import tpu as pltpu
from jax.sharding import Mesh, PartitionSpec as P

BLK = ("yl", "x")
RHS = ("z", "yh", "c")
CHIPS = ("z", "yh")


def exchange(parts, axis):
    return lax.all_to_all(parts, axis, 0, 0, tiled=True)


def repeat(part, count):
    return jnp.broadcast_to(part[None], (count,) + part.shape)


def gather_chips(part):
    got = exchange(repeat(part, lax.axis_size(CHIPS)), CHIPS)
    return jnp.swapaxes(got, 0, 1).reshape(part.shape[0], -1)


def times(values, rows):
    return lax.dot_general(
        values, rows, (((1,), (1,)), ((), ())), preferred_element_type=jnp.float32
    )


def times_exact(values, rows):
    first = lax.reduce_precision(values, 8, 7)
    rest = values - first
    second = lax.reduce_precision(rest, 8, 7)
    third = rest - second
    terms = jnp.concatenate([first, second, third], 0).astype(jnp.bfloat16)
    a, b, c = jnp.split(times(terms, rows), 3, 0)
    return (c + b) + a


TILES = ((1024, 6), (512, 8))


def stream(plan, early_ref, late_ref, held, sems, cases_of):
    slots, tile = held.shape[0], held.shape[3]

    def copy(n):
        index, place = plan[n]
        ref = (late_ref if index else early_ref).at[:, :, place : place + tile]
        return pltpu.make_async_copy(ref, held.at[n % slots], sems.at[n % slots])

    for n in range(min(slots, len(plan))):
        copy(n).start()
    total = [None, None]
    for n, (index, place) in enumerate(plan):
        copy(n).wait()
        part = times(cases_of(place), held[n % slots].reshape(-1, tile))
        total[index] = part if total[index] is None else total[index] + part
        if n + slots < len(plan):
            copy(n + slots).start()
    return total


def first_kernel(plan, *refs):
    *got, early_ref, late_ref, out_ref, held, sems = refs

    def cases_of(place):
        _, chips, _, pair = got[0].shape
        parts = [ref.at[n] for ref in got for n in range(ref.shape[0])]
        part, chip = parts[place // (chips * pair)], place // pair % chips
        return jnp.concatenate([part[chip + n] for n in range(held.shape[3] // pair)], 1)

    total = stream(plan, early_ref, late_ref, held, sems, cases_of)
    for index in range(2):
        out_ref[index] = total[index]


def last_kernel(plan, owner_ref, got, sofar, solved, early_ref, late_ref, out, held, sems):
    pair = got.shape[2]
    xs = solved.shape[0]

    def cases_of(place):
        chip = (place - plan[0][1]) // pair
        return jnp.concatenate([got[chip + n] for n in range(held.shape[3] // pair)], 1)

    total = stream(plan, early_ref, late_ref, held, sems, cases_of)
    owner = owner_ref[0] == 0
    for x in range(xs):
        for index in range(2):
            span = slice(x * pair, (x + 1) * pair)
            value = sofar[index, :, span] + total[index][:, span]
            if index == 0:
                value = jnp.where(owner, solved[x], value)
            for core in range(out.shape[0] // xs):
                out[x * (out.shape[0] // xs) + core, index] = value


def streaming(kernel, span, tiles, early, out_shape, spaces):
    lines, share, _ = early.shape
    tile, slots = tiles
    plan = [(index, place) for place in range(*span, tile) for index in range(2)]
    count = len(plan) * lines * share * tile
    few = out_shape[-2]
    return pl.pallas_call(
        functools.partial(kernel, plan),
        out_shape=jax.ShapeDtypeStruct(out_shape, jnp.float32),
        in_specs=[pl.BlockSpec(memory_space=space) for space in spaces],
        out_specs=pl.BlockSpec(memory_space=pltpu.VMEM),
        scratch_shapes=[
            pltpu.VMEM((slots, lines, share, tile), jnp.bfloat16),
            pltpu.SemaphoreType.DMA((slots,)),
        ],
        compiler_params=pltpu.CompilerParams(vmem_limit_bytes=52 * 2**20),
        cost_estimate=pl.CostEstimate(
            flops=2 * few * count, bytes_accessed=2 * count, transcendentals=0
        ),
    )


def body(factor, loads):
    xs, cores = lax.axis_size("x"), lax.axis_size("c")
    stored, given = factor[:, 0], loads[:, 0]
    share, width = stored.shape[1:]
    cases = given.shape[2]
    block = share * lax.axis_size(RHS)
    steps = width // block
    few = cases // (xs * cores)
    pair = cores * share

    last = width - block
    early = lax.all_gather(stored[0], ("x", "c"), axis=0)
    late = lax.all_gather(stored[1], ("x", "c"), axis=0)

    def panel(row, column):
        part = early[:, :, column * block : (column + 1) * block]
        return part.reshape(xs, pair, block)[row:].reshape(-1, block)

    chips = lax.axis_size(CHIPS)

    together = lax.all_gather(given[0], "c", axis=0, tiled=True).T
    mine = lax.dynamic_index_in_dim(
        together.reshape(xs, cores, few, pair), lax.axis_index("c"), 1, False
    )
    mine = mine.reshape(xs * few, pair)
    start = lax.all_gather(stored[0, :, :block], "c", axis=0, tiled=True)
    whole = gather_chips(mine)
    first = times_exact(whole, start)
    first = jnp.where(lax.axis_index("x") == 0, first, mine)
    state = exchange(first.reshape(xs, few, pair), "x")

    def to_planes(parts):
        got = lax.all_gather(jnp.stack(parts), "yl", axis=0)[0]
        return got, jnp.minimum(jnp.abs(got[0, 0, :1].astype(jnp.float32)), 0.0)

    solved, known, spread = [state[0]], [], []
    state = state[1:]
    for step in range(1, steps):
        part = solved[-1]
        if step + 1 == steps:
            got, none = to_planes(known)
            part, spread = part + none, [got]
            known = []
        got = exchange(repeat(part.astype(jnp.bfloat16), chips), CHIPS)
        known.append(got)
        whole = jnp.swapaxes(got, 0, 1).reshape(few, block)
        update = times(whole, panel(step, step - 1))
        update = update.reshape(few, steps - step, pair)
        state = state - jnp.swapaxes(update, 0, 1)
        solved.append(times_exact(gather_chips(state[0]), panel(step, step)[:pair]))
        state = state[1:]

    got, none = to_planes(known)
    spread.append(got)
    planes = ("yl",) + CHIPS
    got = (solved[-1] + none).astype(jnp.bfloat16)
    got = exchange(repeat(got, lax.axis_size(planes)), planes)
    sofar = streaming(
        first_kernel,
        (0, last),
        TILES[0],
        early,
        (2, few, xs * pair),
        [pltpu.VMEM] * len(spread) + [pl.ANY] * 2,
    )(*spread, early, late)
    both = streaming(
        last_kernel,
        (last, width),
        TILES[1],
        early,
        (xs * cores, 2, few, pair),
        [pltpu.SMEM] + [pltpu.VMEM] * 3 + [pl.ANY] * 2,
    )(lax.axis_index("yl")[None], got, sofar, jnp.stack(solved), early, late)
    back = exchange(both, ("x", "c"))
    owner = lax.axis_index("yl") == 0
    back = jnp.swapaxes(back, 0, 1).reshape(2, cases, pair).transpose(0, 2, 1)
    back = lax.dynamic_slice_in_dim(back, lax.axis_index("c") * share, share, 1)
    top = jnp.where(owner, back[0], given[0] - back[0])
    return jnp.stack([top, given[1] - back[1]])[:, None]


def solution(mesh):
    fine = Mesh(mesh.devices.reshape(4, 4, 8, 2, 2), BLK + RHS)
    spec = P(None, BLK, RHS, None)
    return jax.shard_map(
        body, mesh=fine, in_specs=(spec, spec), out_specs=spec, check_vma=False
    )
```

```python
import functools

import jax
import jax.numpy as jnp
from jax import lax
from jax.experimental import pallas as pl
from jax.experimental.pallas import tpu as pltpu
from jax.sharding import Mesh, PartitionSpec as P

BLK = ("yl", "x")
RHS = ("z", "yh", "c")
CHIPS = ("z", "yh")


def exchange(parts, axis):
    return lax.all_to_all(parts, axis, 0, 0, tiled=True)


def repeat(part, count):
    return jnp.broadcast_to(part[None], (count,) + part.shape)


def gather_chips(part):
    got = exchange(repeat(part, lax.axis_size(CHIPS)), CHIPS)
    return jnp.swapaxes(got, 0, 1).reshape(part.shape[0], -1)


def times(values, rows):
    return lax.dot_general(
        values, rows, (((1,), (1,)), ((), ())), preferred_element_type=jnp.float32
    )


def times_exact(values, rows):
    first = lax.reduce_precision(values, 8, 7)
    rest = values - first
    second = lax.reduce_precision(rest, 8, 7)
    third = rest - second
    terms = jnp.concatenate([first, second, third], 0).astype(jnp.bfloat16)
    a, b, c = jnp.split(times(terms, rows), 3, 0)
    return (c + b) + a


TILES = ((1024, 6), (512, 8))


def stream(plan, early_ref, late_ref, held, sems, cases_of):
    slots, tile = held.shape[0], held.shape[3]

    def copy(n):
        index, place = plan[n]
        ref = (late_ref if index else early_ref).at[:, :, place : place + tile]
        return pltpu.make_async_copy(ref, held.at[n % slots], sems.at[n % slots])

    for n in range(min(slots, len(plan))):
        copy(n).start()
    total = [None, None]
    for n, (index, place) in enumerate(plan):
        copy(n).wait()
        part = times(cases_of(place), held[n % slots].reshape(-1, tile))
        total[index] = part if total[index] is None else total[index] + part
        if n + slots < len(plan):
            copy(n + slots).start()
    return total


def first_kernel(plan, *refs):
    *got, early_ref, late_ref, out_ref, held, sems = refs

    def cases_of(place):
        chips, _, pair = got[0].shape
        part, chip = got[place // (chips * pair)], place // pair % chips
        return jnp.concatenate([part[chip + n] for n in range(held.shape[3] // pair)], 1)

    total = stream(plan, early_ref, late_ref, held, sems, cases_of)
    for index in range(2):
        out_ref[index] = total[index]


def last_kernel(plan, owner_ref, got, sofar, solved, early_ref, late_ref, out, held, sems):
    pair = got.shape[2]
    xs = solved.shape[0]

    def cases_of(place):
        chip = (place - plan[0][1]) // pair
        return jnp.concatenate([got[chip + n] for n in range(held.shape[3] // pair)], 1)

    total = stream(plan, early_ref, late_ref, held, sems, cases_of)
    owner = owner_ref[0] == 0
    for x in range(xs):
        for index in range(2):
            span = slice(x * pair, (x + 1) * pair)
            value = sofar[index, :, span] + total[index][:, span]
            if index == 0:
                value = jnp.where(owner, solved[x], value)
            for core in range(out.shape[0] // xs):
                out[x * (out.shape[0] // xs) + core, index] = value


def streaming(kernel, span, tiles, early, out_shape, spaces):
    lines, share, _ = early.shape
    tile, slots = tiles
    plan = [(index, place) for place in range(*span, tile) for index in range(2)]
    count = len(plan) * lines * share * tile
    few = out_shape[-2]
    return pl.pallas_call(
        functools.partial(kernel, plan),
        out_shape=jax.ShapeDtypeStruct(out_shape, jnp.float32),
        in_specs=[pl.BlockSpec(memory_space=space) for space in spaces],
        out_specs=pl.BlockSpec(memory_space=pltpu.VMEM),
        scratch_shapes=[
            pltpu.VMEM((slots, lines, share, tile), jnp.bfloat16),
            pltpu.SemaphoreType.DMA((slots,)),
        ],
        compiler_params=pltpu.CompilerParams(vmem_limit_bytes=52 * 2**20),
        cost_estimate=pl.CostEstimate(
            flops=2 * few * count, bytes_accessed=2 * count, transcendentals=0
        ),
    )


def body(factor, loads):
    xs, cores = lax.axis_size("x"), lax.axis_size("c")
    stored, given = factor[:, 0], loads[:, 0]
    share, width = stored.shape[1:]
    cases = given.shape[2]
    block = share * lax.axis_size(RHS)
    steps = width // block
    few = cases // (xs * cores)
    pair = cores * share

    last = width - block
    early = lax.all_gather(stored[0], ("x", "c"), axis=0)
    late = lax.all_gather(stored[1], ("x", "c"), axis=0)

    def panel(row, column):
        part = early[:, :, column * block : (column + 1) * block]
        return part.reshape(xs, pair, block)[row:].reshape(-1, block)

    def to_all(part, own_plane=True):
        planes = ("yl",) + CHIPS
        got = exchange(repeat(part, lax.axis_size(planes)), planes)
        return got[: lax.axis_size(CHIPS)] if own_plane else got

    together = lax.all_gather(given[0], "c", axis=0, tiled=True).T
    mine = lax.dynamic_index_in_dim(
        together.reshape(xs, cores, few, pair), lax.axis_index("c"), 1, False
    )
    mine = mine.reshape(xs * few, pair)
    start = lax.all_gather(stored[0, :, :block], "c", axis=0, tiled=True)
    whole = gather_chips(mine)
    first = times_exact(whole, start)
    first = jnp.where(lax.axis_index("x") == 0, first, mine)
    state = exchange(first.reshape(xs, few, pair), "x")

    solved, known = [state[0]], []
    state = state[1:]
    for step in range(1, steps):
        got = to_all(solved[-1].astype(jnp.bfloat16))
        known.append(got)
        whole = jnp.swapaxes(got, 0, 1).reshape(few, block)
        if step == 1:
            first = state[0] - times(whole, panel(step, step - 1)[:pair])
            rest = times(whole, panel(step + 1, step - 1))
        else:
            rest = times(whole, panel(step, step - 1))
            first = state[0] - rest[:, :pair]
            rest = rest[:, pair:]
        solved.append(times_exact(gather_chips(first), panel(step, step)[:pair]))
        rest = rest.reshape(few, steps - step - 1, pair)
        state = state[1:] - jnp.swapaxes(rest, 0, 1)

    got = to_all(solved[-1].astype(jnp.bfloat16), False)
    sofar = streaming(
        first_kernel,
        (0, last),
        TILES[0],
        early,
        (2, few, xs * pair),
        [pltpu.VMEM] * len(known) + [pl.ANY] * 2,
    )(*known, early, late)
    both = streaming(
        last_kernel,
        (last, width),
        TILES[1],
        early,
        (xs * cores, 2, few, pair),
        [pltpu.SMEM] + [pltpu.VMEM] * 3 + [pl.ANY] * 2,
    )(lax.axis_index("yl")[None], got, sofar, jnp.stack(solved), early, late)
    back = exchange(both, ("x", "c"))
    owner = lax.axis_index("yl") == 0
    back = jnp.swapaxes(back, 0, 1).reshape(2, cases, pair).transpose(0, 2, 1)
    back = lax.dynamic_slice_in_dim(back, lax.axis_index("c") * share, share, 1)
    top = jnp.where(owner, back[0], given[0] - back[0])
    return jnp.stack([top, given[1] - back[1]])[:, None]


def solution(mesh):
    fine = Mesh(mesh.devices.reshape(4, 4, 8, 2, 2), BLK + RHS)
    spec = P(None, BLK, RHS, None)
    return jax.shard_map(
        body, mesh=fine, in_specs=(spec, spec), out_specs=spec, check_vma=False
    )
```

```python
import functools

import jax
import jax.numpy as jnp
from jax import lax
from jax.experimental import pallas as pl
from jax.experimental.pallas import tpu as pltpu
from jax.sharding import Mesh, PartitionSpec as P

BLK = ("yl", "x")
RHS = ("z", "yh", "c")
CHIPS = ("z", "yh")


def exchange(parts, axis):
    return lax.all_to_all(parts, axis, 0, 0, tiled=True)


def repeat(part, count):
    return jnp.broadcast_to(part[None], (count,) + part.shape)


def gather_chips(part):
    got = exchange(repeat(part, lax.axis_size(CHIPS)), CHIPS)
    return jnp.swapaxes(got, 0, 1).reshape(part.shape[0], -1)


def times(values, rows):
    return lax.dot_general(
        values, rows, (((1,), (1,)), ((), ())), preferred_element_type=jnp.float32
    )


def times_exact(values, rows):
    first = lax.reduce_precision(values, 8, 7)
    rest = values - first
    second = lax.reduce_precision(rest, 8, 7)
    third = rest - second
    terms = jnp.concatenate([first, second, third], 0).astype(jnp.bfloat16)
    a, b, c = jnp.split(times(terms, rows), 3, 0)
    return (c + b) + a


TILES = ((1024, 6), (512, 8))


def stream(plan, early_ref, late_ref, held, sems, cases_of):
    slots, tile = held.shape[0], held.shape[3]

    def copy(n):
        index, place = plan[n]
        ref = (late_ref if index else early_ref).at[:, :, place : place + tile]
        return pltpu.make_async_copy(ref, held.at[n % slots], sems.at[n % slots])

    for n in range(min(slots, len(plan))):
        copy(n).start()
    total = [None, None]
    for n, (index, place) in enumerate(plan):
        copy(n).wait()
        part = times(cases_of(place), held[n % slots].reshape(-1, tile))
        total[index] = part if total[index] is None else total[index] + part
        if n + slots < len(plan):
            copy(n + slots).start()
    return total


def first_kernel(plan, *refs):
    *got, early_ref, late_ref, out_ref, held, sems = refs

    def cases_of(place):
        chips, _, pair = got[0].shape
        part, chip = got[place // (chips * pair)], place // pair % chips
        return jnp.concatenate([part[chip + n] for n in range(held.shape[3] // pair)], 1)

    total = stream(plan, early_ref, late_ref, held, sems, cases_of)
    for index in range(2):
        out_ref[index] = total[index]


def last_kernel(plan, owner_ref, got, sofar, solved, early_ref, late_ref, out, held, sems):
    pair = got.shape[2]
    xs = solved.shape[0]

    def cases_of(place):
        chip = (place - plan[0][1]) // pair
        return jnp.concatenate([got[chip + n] for n in range(held.shape[3] // pair)], 1)

    total = stream(plan, early_ref, late_ref, held, sems, cases_of)
    owner = owner_ref[0] == 0
    for x in range(xs):
        for index in range(2):
            span = slice(x * pair, (x + 1) * pair)
            value = sofar[index, :, span] + total[index][:, span]
            if index == 0:
                value = jnp.where(owner, solved[x], value)
            for core in range(out.shape[0] // xs):
                out[x * (out.shape[0] // xs) + core, index] = value


def output_kernel(owner_ref, core_ref, back, given, out):
    lines, rounds, few, pair = back.shape
    share = out.shape[1]
    owner, first = owner_ref[0] == 0, core_ref[0] == 0
    for index in range(rounds):
        rows = back[:, index].reshape(lines * few, pair).T
        rows = jnp.where(first, rows[:share], rows[share:])
        value = given[index] - rows
        out[index] = jnp.where(owner, rows, value) if index == 0 else value


def streaming(kernel, span, tiles, early, out_shape, spaces):
    lines, share, _ = early.shape
    tile, slots = tiles
    plan = [(index, place) for place in range(*span, tile) for index in range(2)]
    count = len(plan) * lines * share * tile
    few = out_shape[-2]
    return pl.pallas_call(
        functools.partial(kernel, plan),
        out_shape=jax.ShapeDtypeStruct(out_shape, jnp.float32),
        in_specs=[pl.BlockSpec(memory_space=space) for space in spaces],
        out_specs=pl.BlockSpec(memory_space=pltpu.VMEM),
        scratch_shapes=[
            pltpu.VMEM((slots, lines, share, tile), jnp.bfloat16),
            pltpu.SemaphoreType.DMA((slots,)),
        ],
        compiler_params=pltpu.CompilerParams(vmem_limit_bytes=52 * 2**20),
        cost_estimate=pl.CostEstimate(
            flops=2 * few * count, bytes_accessed=2 * count, transcendentals=0
        ),
    )


def body(factor, loads):
    xs, cores = lax.axis_size("x"), lax.axis_size("c")
    stored, given = factor[:, 0], loads[:, 0]
    share, width = stored.shape[1:]
    cases = given.shape[2]
    block = share * lax.axis_size(RHS)
    steps = width // block
    few = cases // (xs * cores)
    pair = cores * share

    last = width - block
    early = lax.all_gather(stored[0], ("x", "c"), axis=0)
    late = lax.all_gather(stored[1], ("x", "c"), axis=0)

    def panel(row, column):
        part = early[:, :, column * block : (column + 1) * block]
        return part.reshape(xs, pair, block)[row:].reshape(-1, block)

    def to_all(part, own_plane=True):
        planes = ("yl",) + CHIPS
        got = exchange(repeat(part, lax.axis_size(planes)), planes)
        return got[: lax.axis_size(CHIPS)] if own_plane else got

    together = lax.all_gather(given[0], "c", axis=0, tiled=True).T
    mine = lax.dynamic_index_in_dim(
        together.reshape(xs, cores, few, pair), lax.axis_index("c"), 1, False
    )
    mine = mine.reshape(xs * few, pair)
    start = lax.all_gather(stored[0, :, :block], "c", axis=0, tiled=True)
    whole = gather_chips(mine)
    first = times_exact(whole, start)
    first = jnp.where(lax.axis_index("x") == 0, first, mine)
    state = exchange(first.reshape(xs, few, pair), "x")

    solved, known = [state[0]], []
    state = state[1:]
    for step in range(1, steps):
        got = to_all(solved[-1].astype(jnp.bfloat16))
        known.append(got)
        whole = jnp.swapaxes(got, 0, 1).reshape(few, block)
        if step == 1:
            first = state[0] - times(whole, panel(step, step - 1)[:pair])
            rest = times(whole, panel(step + 1, step - 1))
        else:
            rest = times(whole, panel(step, step - 1))
            first = state[0] - rest[:, :pair]
            rest = rest[:, pair:]
        solved.append(times_exact(gather_chips(first), panel(step, step)[:pair]))
        rest = rest.reshape(few, steps - step - 1, pair)
        state = state[1:] - jnp.swapaxes(rest, 0, 1)

    got = to_all(solved[-1].astype(jnp.bfloat16), False)
    sofar = streaming(
        first_kernel,
        (0, last),
        TILES[0],
        early,
        (2, few, xs * pair),
        [pltpu.VMEM] * len(known) + [pl.ANY] * 2,
    )(*known, early, late)
    both = streaming(
        last_kernel,
        (last, width),
        TILES[1],
        early,
        (xs * cores, 2, few, pair),
        [pltpu.SMEM] + [pltpu.VMEM] * 3 + [pl.ANY] * 2,
    )(lax.axis_index("yl")[None], got, sofar, jnp.stack(solved), early, late)
    back = exchange(both, ("x", "c"))
    result = pl.pallas_call(
        output_kernel,
        out_shape=jax.ShapeDtypeStruct(given.shape, jnp.float32),
        in_specs=[pl.BlockSpec(memory_space=pltpu.SMEM)] * 2
        + [pl.BlockSpec(memory_space=pltpu.VMEM)] * 2,
        out_specs=pl.BlockSpec(memory_space=pltpu.VMEM),
    )(lax.axis_index("yl")[None], lax.axis_index("c")[None], back, given)
    return result[:, None]


def solution(mesh):
    fine = Mesh(mesh.devices.reshape(4, 4, 8, 2, 2), BLK + RHS)
    spec = P(None, BLK, RHS, None)
    return jax.shard_map(
        body, mesh=fine, in_specs=(spec, spec), out_specs=spec, check_vma=False
    )
```

```python
import functools

import jax
import jax.numpy as jnp
from jax import lax
from jax.experimental import pallas as pl
from jax.experimental.pallas import tpu as pltpu
from jax.sharding import Mesh, PartitionSpec as P

BLK = ("yl", "x")
RHS = ("z", "yh", "c")
CHIPS = ("z", "yh")


def exchange(parts, axis):
    return lax.all_to_all(parts, axis, 0, 0, tiled=True)


def repeat(part, count):
    return jnp.broadcast_to(part[None], (count,) + part.shape)


def gather_chips(part):
    got = exchange(repeat(part, lax.axis_size(CHIPS)), CHIPS)
    return jnp.swapaxes(got, 0, 1).reshape(part.shape[0], -1)


def times(values, rows):
    return lax.dot_general(
        values, rows, (((1,), (1,)), ((), ())), preferred_element_type=jnp.float32
    )


def times_exact(values, rows):
    first = lax.reduce_precision(values, 8, 7)
    rest = values - first
    second = lax.reduce_precision(rest, 8, 7)
    third = rest - second
    terms = jnp.concatenate([first, second, third], 0).astype(jnp.bfloat16)
    a, b, c = jnp.split(times(terms, rows), 3, 0)
    return (c + b) + a


TILES = ((1024, 6), (512, 8))


def stream(plan, early_ref, late_ref, held, sems, cases_of):
    slots, tile = held.shape[0], held.shape[3]

    def copy(n):
        index, place = plan[n]
        ref = (late_ref if index else early_ref).at[:, :, place : place + tile]
        return pltpu.make_async_copy(ref, held.at[n % slots], sems.at[n % slots])

    for n in range(min(slots, len(plan))):
        copy(n).start()
    total = [None, None]
    for n, (index, place) in enumerate(plan):
        copy(n).wait()
        part = times(cases_of(place), held[n % slots].reshape(-1, tile))
        total[index] = part if total[index] is None else total[index] + part
        if n + slots < len(plan):
            copy(n + slots).start()
    return total


def first_kernel(plan, *refs):
    *got, early_ref, late_ref, out_ref, held, sems = refs

    def cases_of(place):
        chips, _, pair = got[0].shape
        part, chip = got[place // (chips * pair)], place // pair % chips
        return jnp.concatenate([part[chip + n] for n in range(held.shape[3] // pair)], 1)

    total = stream(plan, early_ref, late_ref, held, sems, cases_of)
    for index in range(2):
        out_ref[index] = total[index]


def last_kernel(plan, owner_ref, got, sofar, solved, early_ref, late_ref, out, held, sems):
    pair = got.shape[2]
    xs = solved.shape[0]

    def cases_of(place):
        chip = (place - plan[0][1]) // pair
        return jnp.concatenate([got[chip + n] for n in range(held.shape[3] // pair)], 1)

    total = stream(plan, early_ref, late_ref, held, sems, cases_of)
    owner = owner_ref[0] == 0
    for x in range(xs):
        for index in range(2):
            span = slice(x * pair, (x + 1) * pair)
            value = sofar[index, :, span] + total[index][:, span]
            if index == 0:
                value = jnp.where(owner, solved[x], value)
            for core in range(out.shape[0] // xs):
                out[x * (out.shape[0] // xs) + core, index] = value


def output_kernel(owner_ref, core_ref, back, given, out):
    lines, rounds, few, pair = back.shape
    share = out.shape[1]
    owner, first = owner_ref[0] == 0, core_ref[0] == 0
    for index in range(rounds):
        rows = back[:, index].reshape(lines * few, pair).T
        rows = jnp.where(first, rows[:share], rows[share:])
        value = given[index] - rows
        out[index] = jnp.where(owner, rows, value) if index == 0 else value


def streaming(kernel, span, tiles, early, out_shape, spaces):
    lines, share, _ = early.shape
    tile, slots = tiles
    plan = [(index, place) for place in range(*span, tile) for index in range(2)]
    count = len(plan) * lines * share * tile
    few = out_shape[-2]
    return pl.pallas_call(
        functools.partial(kernel, plan),
        out_shape=jax.ShapeDtypeStruct(out_shape, jnp.float32),
        in_specs=[pl.BlockSpec(memory_space=space) for space in spaces],
        out_specs=pl.BlockSpec(memory_space=pltpu.VMEM),
        scratch_shapes=[
            pltpu.VMEM((slots, lines, share, tile), jnp.bfloat16),
            pltpu.SemaphoreType.DMA((slots,)),
        ],
        compiler_params=pltpu.CompilerParams(vmem_limit_bytes=52 * 2**20),
        cost_estimate=pl.CostEstimate(
            flops=2 * few * count, bytes_accessed=2 * count, transcendentals=0
        ),
    )


def body(factor, loads):
    xs, cores = lax.axis_size("x"), lax.axis_size("c")
    stored, given = factor[:, 0], loads[:, 0]
    share, width = stored.shape[1:]
    cases = given.shape[2]
    block = share * lax.axis_size(RHS)
    steps = width // block
    few = cases // (xs * cores)
    pair = cores * share

    last = width - block
    early = lax.all_gather(stored[0], ("x", "c"), axis=0)
    late = lax.all_gather(stored[1], ("x", "c"), axis=0)

    def panel(row, column):
        part = early[:, :, column * block : (column + 1) * block]
        return part.reshape(xs, pair, block)[row:].reshape(-1, block)

    def to_all(part, own_plane=True):
        planes = ("yl",) + CHIPS
        got = exchange(repeat(part, lax.axis_size(planes)), planes)
        return got[: lax.axis_size(CHIPS)] if own_plane else got

    together = lax.all_gather(given[0], "c", axis=0, tiled=True).T
    mine = lax.dynamic_index_in_dim(
        together.reshape(xs, cores, few, pair), lax.axis_index("c"), 1, False
    )
    mine = mine.reshape(xs * few, pair)
    start = lax.all_gather(stored[0, :, :block], "c", axis=0, tiled=True)
    whole = gather_chips(mine)
    first = times_exact(whole, start)
    first = jnp.where(lax.axis_index("x") == 0, first, mine)
    state = exchange(first.reshape(xs, few, pair), "x")

    solved, known = [state[0]], []
    state = state[1:]
    for step in range(1, steps):
        got = to_all(solved[-1].astype(jnp.bfloat16))
        known.append(got)
        whole = jnp.swapaxes(got, 0, 1).reshape(few, block)
        if step == 1:
            first = state[0] - times(whole, panel(step, step - 1)[:pair])
            early, first = lax.optimization_barrier((early, first))
            rest = times(whole, panel(step + 1, step - 1))
        else:
            rest = times(whole, panel(step, step - 1))
            first = state[0] - rest[:, :pair]
            rest = rest[:, pair:]
        solved.append(times_exact(gather_chips(first), panel(step, step)[:pair]))
        rest = rest.reshape(few, steps - step - 1, pair)
        state = state[1:] - jnp.swapaxes(rest, 0, 1)

    got = to_all(solved[-1].astype(jnp.bfloat16), False)
    sofar = streaming(
        first_kernel,
        (0, last),
        TILES[0],
        early,
        (2, few, xs * pair),
        [pltpu.VMEM] * len(known) + [pl.ANY] * 2,
    )(*known, early, late)
    both = streaming(
        last_kernel,
        (last, width),
        TILES[1],
        early,
        (xs * cores, 2, few, pair),
        [pltpu.SMEM] + [pltpu.VMEM] * 3 + [pl.ANY] * 2,
    )(lax.axis_index("yl")[None], got, sofar, jnp.stack(solved), early, late)
    back = exchange(both, ("x", "c"))
    result = pl.pallas_call(
        output_kernel,
        out_shape=jax.ShapeDtypeStruct(given.shape, jnp.float32),
        in_specs=[pl.BlockSpec(memory_space=pltpu.SMEM)] * 2
        + [pl.BlockSpec(memory_space=pltpu.VMEM)] * 2,
        out_specs=pl.BlockSpec(memory_space=pltpu.VMEM),
    )(lax.axis_index("yl")[None], lax.axis_index("c")[None], back, given)
    return result[:, None]


def solution(mesh):
    fine = Mesh(mesh.devices.reshape(4, 4, 8, 2, 2), BLK + RHS)
    spec = P(None, BLK, RHS, None)
    return jax.shard_map(
        body, mesh=fine, in_specs=(spec, spec), out_specs=spec, check_vma=False
    )
```

```python
import functools

import jax
import jax.numpy as jnp
from jax import lax
from jax.experimental import pallas as pl
from jax.experimental.pallas import tpu as pltpu
from jax.sharding import Mesh, PartitionSpec as P

BLK = ("yl", "x")
RHS = ("z", "yh", "c")
CHIPS = ("z", "yh")


def exchange(parts, axis):
    return lax.all_to_all(parts, axis, 0, 0, tiled=True)


def repeat(part, count):
    return jnp.broadcast_to(part[None], (count,) + part.shape)


def gather_chips(part):
    got = exchange(repeat(part, lax.axis_size(CHIPS)), CHIPS)
    return jnp.swapaxes(got, 0, 1).reshape(part.shape[0], -1)


def times(values, rows):
    return lax.dot_general(
        values, rows, (((1,), (1,)), ((), ())), preferred_element_type=jnp.float32
    )


def times_exact(values, rows):
    first = lax.reduce_precision(values, 8, 7)
    rest = values - first
    second = lax.reduce_precision(rest, 8, 7)
    third = rest - second
    terms = jnp.concatenate([first, second, third], 0).astype(jnp.bfloat16)
    a, b, c = jnp.split(times(terms, rows), 3, 0)
    return (c + b) + a


TILES = ((1024, 6), (256, 16))


def stream(plan, early_ref, late_ref, held, sems, cases_of):
    slots, tile = held.shape[0], held.shape[3]

    def copy(n):
        index, place = plan[n]
        ref = (late_ref if index else early_ref).at[:, :, place : place + tile]
        return pltpu.make_async_copy(ref, held.at[n % slots], sems.at[n % slots])

    for n in range(min(slots, len(plan))):
        copy(n).start()
    total = [None, None]
    for n, (index, place) in enumerate(plan):
        copy(n).wait()
        part = times(cases_of(place), held[n % slots].reshape(-1, tile))
        total[index] = part if total[index] is None else total[index] + part
        if n + slots < len(plan):
            copy(n + slots).start()
    return total


def first_kernel(plan, *refs):
    *got, early_ref, late_ref, out_ref, held, sems = refs

    def cases_of(place):
        chips, _, pair = got[0].shape
        part, chip = got[place // (chips * pair)], place // pair % chips
        return jnp.concatenate([part[chip + n] for n in range(held.shape[3] // pair)], 1)

    total = stream(plan, early_ref, late_ref, held, sems, cases_of)
    for index in range(2):
        out_ref[index] = total[index]


def last_kernel(plan, owner_ref, got, sofar, solved, early_ref, late_ref, out, held, sems):
    pair = got.shape[2]
    xs = solved.shape[0]

    def cases_of(place):
        chip = (place - plan[0][1]) // pair
        return jnp.concatenate([got[chip + n] for n in range(held.shape[3] // pair)], 1)

    total = stream(plan, early_ref, late_ref, held, sems, cases_of)
    owner = owner_ref[0] == 0
    for x in range(xs):
        for index in range(2):
            span = slice(x * pair, (x + 1) * pair)
            value = sofar[index, :, span] + total[index][:, span]
            if index == 0:
                value = jnp.where(owner, solved[x], value)
            for core in range(out.shape[0] // xs):
                out[x * (out.shape[0] // xs) + core, index] = value


def output_kernel(owner_ref, core_ref, back, given, out):
    lines, rounds, few, pair = back.shape
    share = out.shape[1]
    owner, first = owner_ref[0] == 0, core_ref[0] == 0
    for index in range(rounds):
        rows = back[:, index].reshape(lines * few, pair).T
        rows = jnp.where(first, rows[:share], rows[share:])
        value = given[index] - rows
        out[index] = jnp.where(owner, rows, value) if index == 0 else value


def streaming(kernel, span, tiles, early, out_shape, spaces):
    lines, share, _ = early.shape
    tile, slots = tiles
    plan = [(index, place) for place in range(*span, tile) for index in range(2)]
    count = len(plan) * lines * share * tile
    few = out_shape[-2]
    return pl.pallas_call(
        functools.partial(kernel, plan),
        out_shape=jax.ShapeDtypeStruct(out_shape, jnp.float32),
        in_specs=[pl.BlockSpec(memory_space=space) for space in spaces],
        out_specs=pl.BlockSpec(memory_space=pltpu.VMEM),
        scratch_shapes=[
            pltpu.VMEM((slots, lines, share, tile), jnp.bfloat16),
            pltpu.SemaphoreType.DMA((slots,)),
        ],
        compiler_params=pltpu.CompilerParams(vmem_limit_bytes=52 * 2**20),
        cost_estimate=pl.CostEstimate(
            flops=2 * few * count, bytes_accessed=2 * count, transcendentals=0
        ),
    )


def body(factor, loads):
    xs, cores = lax.axis_size("x"), lax.axis_size("c")
    stored, given = factor[:, 0], loads[:, 0]
    share, width = stored.shape[1:]
    cases = given.shape[2]
    block = share * lax.axis_size(RHS)
    steps = width // block
    few = cases // (xs * cores)
    pair = cores * share

    last = width - block
    early = lax.all_gather(stored[0], ("x", "c"), axis=0)
    late = lax.all_gather(stored[1], ("x", "c"), axis=0)

    def panel(row, column):
        part = early[:, :, column * block : (column + 1) * block]
        return part.reshape(xs, pair, block)[row:].reshape(-1, block)

    def to_all(part, own_plane=True):
        planes = ("yl",) + CHIPS
        got = exchange(repeat(part, lax.axis_size(planes)), planes)
        return got[: lax.axis_size(CHIPS)] if own_plane else got

    together = lax.all_gather(given[0], "c", axis=0, tiled=True).T
    mine = lax.dynamic_index_in_dim(
        together.reshape(xs, cores, few, pair), lax.axis_index("c"), 1, False
    )
    mine = mine.reshape(xs * few, pair)
    start = lax.all_gather(stored[0, :, :block], "c", axis=0, tiled=True)
    whole = gather_chips(mine)
    first = times_exact(whole, start)
    first = jnp.where(lax.axis_index("x") == 0, first, mine)
    state = exchange(first.reshape(xs, few, pair), "x")

    solved, known = [state[0]], []
    state = state[1:]
    for step in range(1, steps):
        got = to_all(solved[-1].astype(jnp.bfloat16))
        known.append(got)
        whole = jnp.swapaxes(got, 0, 1).reshape(few, block)
        if step == 1:
            first = state[0] - times(whole, panel(step, step - 1)[:pair])
            early, first = lax.optimization_barrier((early, first))
            rest = times(whole, panel(step + 1, step - 1))
        else:
            rest = times(whole, panel(step, step - 1))
            first = state[0] - rest[:, :pair]
            rest = rest[:, pair:]
        solved.append(times_exact(gather_chips(first), panel(step, step)[:pair]))
        rest = rest.reshape(few, steps - step - 1, pair)
        state = state[1:] - jnp.swapaxes(rest, 0, 1)

    got = to_all(solved[-1].astype(jnp.bfloat16), False)
    sofar = streaming(
        first_kernel,
        (0, last),
        TILES[0],
        early,
        (2, few, xs * pair),
        [pltpu.VMEM] * len(known) + [pl.ANY] * 2,
    )(*known, early, late)
    both = streaming(
        last_kernel,
        (last, width),
        TILES[1],
        early,
        (xs * cores, 2, few, pair),
        [pltpu.SMEM] + [pltpu.VMEM] * 3 + [pl.ANY] * 2,
    )(lax.axis_index("yl")[None], got, sofar, jnp.stack(solved), early, late)
    back = exchange(both, ("x", "c"))
    result = pl.pallas_call(
        output_kernel,
        out_shape=jax.ShapeDtypeStruct(given.shape, jnp.float32),
        in_specs=[pl.BlockSpec(memory_space=pltpu.SMEM)] * 2
        + [pl.BlockSpec(memory_space=pltpu.VMEM)] * 2,
        out_specs=pl.BlockSpec(memory_space=pltpu.VMEM),
    )(lax.axis_index("yl")[None], lax.axis_index("c")[None], back, given)
    return result[:, None]


def solution(mesh):
    fine = Mesh(mesh.devices.reshape(4, 4, 8, 2, 2), BLK + RHS)
    spec = P(None, BLK, RHS, None)
    return jax.shard_map(
        body, mesh=fine, in_specs=(spec, spec), out_specs=spec, check_vma=False
    )
```
